128 devices in a mesh: group: 4 (over x), chan: 32 (over y, z, core).
Axes of the slice: x: 4, y: 4, z: 4, core: 2. Of those that a mesh axis runs over, the one named last changes fastest.
Arguments:
- generator: bfloat16 [256, 768, 768], P(('group', 'chan')), may hold values from -0.21875 to 0.21875
- hamiltonian: bfloat16 [256, 768, 768], P(('group', 'chan')), may hold values from -6 to 6
- pair_weight: float32 [256, 768], P(('group', 'chan')), may hold values from -1 to 1
- cross_weight: float32 [256, 768], P(('group', 'chan')), may hold values from -1 to 1
- channel_size: int32 [256], P(('group', 'chan')), may hold values from 1 to 768, as said below
- send_table: int32 [128, 1664], P(('group', 'chan')), may hold values from 0 to 1152, as said below
- receive_table: int32 [128, 1664], P(('group', 'chan')), may hold values from 0 to 1152, as said below
Outputs:
- new_hamiltonian: float32 [256, 768, 768], P(('group', 'chan'))
The draws below stay inside these ranges and needn't reach their ends.
Inputs may be any that keep to these rules, and one draw needn't show every extreme that they name: `channel_size`: at least one channel has exactly 768. `send_table`: value 1152 marks an empty slot; in each device's row the filled slots toward one destination come first and name every local tile exactly once; some pair of devices uses all 13 slots. `receive_table`: value 1152 marks an empty slot; slot (s, k) of device r is filled exactly when slot (r, k) of device s in send_table is; the filled slots name every local particle-hole tile exactly once.
All inputs are finite; a program needn't handle non-finite values.
Results may differ from the reference program's by a relative error of at most 0.0011.
Values may be sent and summed in bfloat16 or wider, within the bound.
No kernel may reach another device: no remote copies, remote signals or barrier semaphores. Data moves between devices by JAX's collectives and lax.ppermute only.
A program may use at most 128 MiB of HBM per device.

```python
import jax
import jax.numpy as jnp
from jax import lax

DIM = 768
TILE = 32
CH_DEV = 2
CHANNELS = 256
DEVICES = 128


def permute_tiles(subkey):
    return jax.random.permutation(subkey, CH_DEV * (DIM // TILE) ** 2).astype(jnp.int32)


def routing_tables(key):
    devices = DEVICES
    tile_count = CH_DEV * (DIM // TILE) ** 2
    even_share = tile_count // devices
    half_share = even_share // 2
    capacity = even_share + half_share
    half_devices = devices // 2
    key_list = jax.random.split(jax.random.fold_in(key, 4242), 4)
    shifts = jax.random.randint(key_list[0], (half_devices,), -half_share, half_share + 1)
    shifts = shifts.at[1].set(half_share)
    offset_counts = jnp.concatenate([even_share + shifts, even_share - shifts]).astype(jnp.int32)
    placing = jax.random.permutation(key_list[1], devices)
    device_rank = jnp.argsort(placing).astype(jnp.int32)
    counts = offset_counts[(device_rank[None, :] - device_rank[:, None]) % devices]
    slot_index = jnp.arange(capacity, dtype=jnp.int32)
    send_perm = jax.vmap(permute_tiles)(jax.random.split(key_list[2], devices))
    send_start = jnp.cumsum(counts, axis=1) - counts
    positions = jnp.clip(send_start[:, :, None] + slot_index, 0, tile_count - 1).reshape(devices, -1)
    picked = jnp.take_along_axis(send_perm, positions, axis=1).reshape(devices, devices, capacity)
    send_out = jnp.where(slot_index < counts[:, :, None], picked, tile_count).reshape(devices, devices * capacity)
    flipped = counts.T
    receive_perm = jax.vmap(permute_tiles)(jax.random.split(key_list[3], devices))
    receive_start = jnp.cumsum(flipped, axis=1) - flipped
    places = jnp.clip(receive_start[:, :, None] + slot_index, 0, tile_count - 1).reshape(devices, -1)
    chosen = jnp.take_along_axis(receive_perm, places, axis=1).reshape(devices, devices, capacity)
    receive_out = jnp.where(slot_index < flipped[:, :, None], chosen, tile_count).reshape(devices, devices * capacity)
    return (send_out.astype(jnp.int32), receive_out.astype(jnp.int32))


def draw_send_table(key, part):
    return routing_tables(key)[0]


def draw_receive_table(key, part):
    return routing_tables(key)[1]


def draw_channel_size(key, part):
    key_list = jax.random.split(jax.random.fold_in(key, 77), 2)
    lengths = jax.random.randint(key_list[0], (CH_DEV * DEVICES,), DIM // 4, DIM + 1)
    chosen = jax.random.randint(key_list[1], (), 0, CH_DEV * DEVICES)
    return lengths.at[chosen].set(DIM).astype(jnp.int32)


def shard_levels(stream_key, shape, shards, low, top_value):
    def one(dim, blocks):
        draws = jax.random.uniform(jax.random.fold_in(jax.random.fold_in(stream_key, 6), dim), (blocks,), jnp.float32, low / len(shards), top_value / len(shards))
        return jnp.repeat(jnp.exp(draws), shape[dim] // blocks).reshape((-1,) + (1,) * (len(shape) - dim - 1))

    loudness = one(*shards[0])
    for cut in shards[1:]:
        loudness = loudness * one(*cut)
    return loudness


def bell_draw(own_key, shape, scale, bound, cuts=(), kind=jnp.bfloat16):
    factor_of = shard_levels(own_key, shape, cuts, -0.22, 0.18) if cuts else 1.0
    drawn = jax.random.normal(own_key, shape, jnp.float32) * scale * factor_of
    return jnp.minimum(jnp.maximum(drawn, -bound), bound).astype(kind)


def setup_inputs(seed: int = 0) -> dict:
    streams_of = jax.random.split(jax.random.key(seed), 8)
    return {
        "generator": bell_draw(streams_of[0], (CHANNELS, DIM, DIM), DIM ** -0.5, 0.21875, ((0, 128),)),
        "hamiltonian": bell_draw(streams_of[1], (CHANNELS, DIM, DIM), 1.0, 6.0, ((0, 128),)),
        "pair_weight": jnp.clip(jax.random.uniform(streams_of[2], (CHANNELS, DIM), jnp.float32, -1.0, 1.0) * shard_levels(streams_of[2], (CHANNELS, DIM), ((0, 128),), -0.4, 0.0), -1.0, 1.0),
        "cross_weight": jnp.clip(jax.random.uniform(streams_of[3], (CHANNELS, DIM), jnp.float32, -1.0, 1.0) * shard_levels(streams_of[3], (CHANNELS, DIM), ((0, 128),), -0.4, 0.0), -1.0, 1.0),
        "channel_size": draw_channel_size(jax.random.fold_in(streams_of[7], 71), 0),
        "send_table": draw_send_table(jax.random.fold_in(streams_of[7], 71), 0),
        "receive_table": draw_receive_table(jax.random.fold_in(streams_of[7], 71), 0),
    }


flow_step = 0.5


def to_tiles(matrices):
    return matrices.reshape(-1, TILE * TILE)


def from_tiles(tile_rows, amount, extent):
    return tile_rows.reshape(amount, extent, extent)


def masked_one(operands):
    matrix, length = operands
    inside = (jnp.arange(matrix.shape[0], dtype=jnp.int32) < length).astype(jnp.float32)
    return (matrix.astype(jnp.float32) * inside[:, None] * inside[None, :]).astype(jnp.bfloat16)


def commute_one(operands):
    former, latter, weight = operands
    latter_weighted = (weight[:, None] * latter.astype(jnp.float32)).astype(jnp.bfloat16)
    former_weighted = (weight[:, None] * former.astype(jnp.float32)).astype(jnp.bfloat16)
    return jnp.dot(former, latter_weighted, preferred_element_type=jnp.float32) - jnp.dot(latter, former_weighted, preferred_element_type=jnp.float32)


def finish(operands):
    ham_one, ladder_one, back_one, length = operands
    inside = (jnp.arange(ham_one.shape[0], dtype=jnp.int32) < length).astype(jnp.float32)
    summed = ham_one.astype(jnp.float32) + flow_step * (ladder_one + back_one.astype(jnp.float32))
    return summed * inside[:, None] * inside[None, :]


def reference(generator, hamiltonian, pair_weight, cross_weight, channel_size, send_table, receive_table):
    channels, extent, _ = generator.shape
    devices = send_table.shape[0]
    capacity = send_table.shape[1] // devices
    tile_count = (channels // devices) * (extent // TILE) ** 2
    tile_total = devices * tile_count
    masked_generator = lax.map(masked_one, (generator, channel_size))
    masked_hamiltonian = lax.map(masked_one, (hamiltonian, channel_size))
    ladder = lax.map(commute_one, (masked_generator, masked_hamiltonian, pair_weight))
    send_three = send_table.reshape(devices, devices, capacity)
    receive_three = receive_table.reshape(devices, devices, capacity).transpose(1, 0, 2)
    filled = send_three < tile_count
    sender = jnp.arange(devices, dtype=jnp.int32)[:, None, None]
    target = jnp.arange(devices, dtype=jnp.int32)[None, :, None]
    source_ids = jnp.where(filled, sender * tile_count + send_three, tile_total).reshape(-1).astype(jnp.int32)
    place_ids = jnp.where(filled, target * tile_count + receive_three, tile_total).reshape(-1).astype(jnp.int32)
    source_of = jnp.zeros((tile_total + 1,), jnp.int32).at[place_ids].set(source_ids)[:tile_total]
    place_of = jnp.zeros((tile_total + 1,), jnp.int32).at[source_ids].set(place_ids)[:tile_total]
    cross_generator = from_tiles(to_tiles(masked_generator)[source_of], channels, extent)
    cross_hamiltonian = from_tiles(to_tiles(masked_hamiltonian)[source_of], channels, extent)
    crossed = lax.map(commute_one, (cross_generator, cross_hamiltonian, cross_weight)).astype(jnp.bfloat16)
    returned = from_tiles(to_tiles(crossed)[place_of], channels, extent)
    return lax.map(finish, (masked_hamiltonian, ladder, returned, channel_size))
```

```python
import functools

import jax
import jax.numpy as jnp
from jax import lax
from jax.experimental import pallas as pl
from jax.experimental.pallas import tpu as pltpu
from jax.sharding import PartitionSpec as P

TILE = 32
LANES = 128
TROWS = TILE * TILE // LANES
ROWS = 16

flow_step = 0.5

VMEM_LIMIT = 60 * 1024 * 1024
AXES = ("group", "chan")


def params():
    return pltpu.CompilerParams(vmem_limit_bytes=VMEM_LIMIT)


def chunks_of(total, count):
    while total % count:
        count -= 1
    return count, total // count


def loop(count, body, unroll=1):
    lax.fori_loop(0, count, lambda i, _: (body(i), 0)[1], 0, unroll=unroll)


def inside_of(first_row, rows, columns, size):
    row = lax.broadcasted_iota(jnp.int32, (rows, columns), 0) + first_row
    column = lax.broadcasted_iota(jnp.int32, (rows, columns), 1)
    return (row < size) & (column < size)


def spread(weight_row, out_ref):
    extent = weight_row.shape[1]
    for k in range(extent // LANES):
        piece = weight_row[:, k * LANES : (k + 1) * LANES]
        out_ref[k * LANES : (k + 1) * LANES, :] = jnp.transpose(
            jnp.broadcast_to(piece, (LANES, LANES))
        )


def pack_kernel(size_ref, table_ref, gen_hbm, ham_hbm, out_hbm, gen, ham, gen_rows, ham_rows, out, in_sem, out_sem):
    channels, extent, _ = gen.shape
    slots = out.shape[0]
    panels = extent // LANES
    parts, part_rows = chunks_of(extent, 2)
    out_parts, out_slots = chunks_of(slots, out_sem.shape[0])

    def loads(c, h):
        at = pl.ds(h * part_rows, part_rows)
        k = c * parts + h
        return (
            pltpu.make_async_copy(gen_hbm.at[c, at], gen.at[c, at], in_sem.at[0, k]),
            pltpu.make_async_copy(ham_hbm.at[c, at], ham.at[c, at], in_sem.at[1, k]),
        )

    for c in range(channels):
        for h in range(parts):
            for copy in loads(c, h):
                copy.start()
    for c in range(channels):
        size = size_ref[c]
        for h in range(parts):
            for copy in loads(c, h):
                copy.wait()

            def block(b, c=c, h=h, size=size):
                first = pl.multiple_of(h * part_rows + b * ROWS, ROWS)
                inside = inside_of(first, ROWS, extent, size)
                base = (c * extent + first) * panels
                for source, target in ((gen, gen_rows), (ham, ham_rows)):
                    values = source[c, pl.ds(first, ROWS), :].astype(jnp.float32)
                    values = jnp.where(inside, values, 0.0)
                    for p in range(panels):
                        target[pl.ds(base + p, ROWS, stride=panels), :] = values[
                            :, p * LANES : (p + 1) * LANES
                        ]

            loop(part_rows // ROWS, block, unroll=2)

    def store(q):
        at = pl.ds(q * out_slots, out_slots)
        return pltpu.make_async_copy(out.at[at], out_hbm.at[at], out_sem.at[q])

    for q in range(out_parts):

        def pick(j, q=q):
            slot = q * out_slots + j
            at = pl.ds(pl.multiple_of(table_ref[0, slot] * TROWS, TROWS), TROWS)
            out[slot] = jnp.concatenate([gen_rows[at, :], ham_rows[at, :]], axis=0).astype(
                jnp.bfloat16
            )

        loop(out_slots, pick, unroll=16)
        store(q).start()
    for q in range(out_parts):
        store(q).wait()


def cross_kernel(table_ref, weight_ref, in_hbm, out_hbm, arrived, gen_rows, ham_rows, gen, ham, wgen, wham, spread_weight, crossed_rows, out, in_sem, out_sem):
    channels, extent = weight_ref.shape
    slots = out.shape[0]
    panels = extent // LANES
    parts, part_slots = chunks_of(slots, in_sem.shape[0])

    def load(q):
        at = pl.ds(q * part_slots, part_slots)
        return pltpu.make_async_copy(in_hbm.at[at], arrived.at[at], in_sem.at[q])

    for q in range(parts):
        load(q).start()
    for c in range(channels):
        spread(weight_ref[c : c + 1, :], spread_weight.at[c])
    for q in range(parts):
        load(q).wait()

        def place(j, q=q):
            slot = q * part_slots + j
            at = pl.ds(pl.multiple_of(table_ref[0, slot] * TROWS, TROWS), TROWS)
            both = arrived[slot].astype(jnp.float32)
            gen_rows[at, :] = both[:TROWS]
            ham_rows[at, :] = both[TROWS:]

        loop(part_slots, place, unroll=16)
    for c in range(channels):

        def block(b, c=c):
            first = pl.multiple_of(b * ROWS, ROWS)
            rows = pl.ds(first, ROWS)
            base = (c * extent + first) * panels
            weight = spread_weight[c, rows, :]
            for p in range(panels):
                lanes = slice(p * LANES, (p + 1) * LANES)
                g = gen_rows[pl.ds(base + p, ROWS, stride=panels), :]
                h = ham_rows[pl.ds(base + p, ROWS, stride=panels), :]
                gen[rows, lanes] = g.astype(jnp.bfloat16)
                ham[rows, lanes] = h.astype(jnp.bfloat16)
                wgen[rows, lanes] = (weight * g).astype(jnp.bfloat16)
                wham[rows, lanes] = (weight * h).astype(jnp.bfloat16)

        loop(extent // ROWS, block, unroll=2)
        wide = 2 * LANES
        for n in range(extent // wide):
            columns = slice(n * wide, (n + 1) * wide)
            first = jnp.dot(gen[...], wham[:, columns], preferred_element_type=jnp.float32)
            second = jnp.dot(ham[...], wgen[:, columns], preferred_element_type=jnp.float32)
            product = first - second
            for i in range(wide // LANES):
                p = n * (wide // LANES) + i
                crossed_rows[
                    pl.ds(c * extent * panels + p, extent, stride=panels), :
                ] = product[:, i * LANES : (i + 1) * LANES]

    def store(q):
        at = pl.ds(q * part_slots, part_slots)
        return pltpu.make_async_copy(out.at[at], out_hbm.at[at], out_sem.at[q])

    for q in range(parts):

        def pick(j, q=q):
            slot = q * part_slots + j
            at = pl.ds(pl.multiple_of(table_ref[0, slot] * TROWS, TROWS), TROWS)
            out[slot] = crossed_rows[at, :].astype(jnp.bfloat16)

        loop(part_slots, pick, unroll=16)
        store(q).start()
    for q in range(parts):
        store(q).wait()


def ladder_kernel(size_ref, weight_ref, gen_ref, ham_ref, out_ref, gen, ham, wgen, wham, spread_weight):
    extent = gen_ref.shape[1]
    c = pl.program_id(0)
    size = size_ref[c]
    spread(weight_ref[0], spread_weight)

    def block(b):
        rows = pl.ds(pl.multiple_of(b * ROWS, ROWS), ROWS)
        inside = inside_of(b * ROWS, ROWS, extent, size)
        weight = jnp.tile(spread_weight[rows, :], (1, extent // LANES))
        g = jnp.where(inside, gen_ref[0, rows, :].astype(jnp.float32), 0.0)
        h = jnp.where(inside, ham_ref[0, rows, :].astype(jnp.float32), 0.0)
        gen[rows, :] = g.astype(jnp.bfloat16)
        ham[rows, :] = h.astype(jnp.bfloat16)
        wgen[rows, :] = (weight * g).astype(jnp.bfloat16)
        wham[rows, :] = (weight * h).astype(jnp.bfloat16)

    loop(extent // ROWS, block)
    wide = 2 * LANES
    for n in range(extent // wide):
        columns = slice(n * wide, (n + 1) * wide)
        first = jnp.dot(gen[...], wham[:, columns], preferred_element_type=jnp.float32)
        second = jnp.dot(ham[...], wgen[:, columns], preferred_element_type=jnp.float32)
        out_ref[0, :, columns] = ham[:, columns].astype(jnp.float32) + flow_step * (first - second)


def finish_kernel(size_ref, table_ref, base_hbm, in_hbm, out_hbm, base, arrived, rows_back, out, base_sem, in_sem, out_sem):
    channels, extent, _ = base.shape
    slots = arrived.shape[0]
    panels = extent // LANES
    parts, part_slots = chunks_of(slots, in_sem.shape[0])
    cuts, cut_rows = chunks_of(extent, 4)

    def load(q):
        at = pl.ds(q * part_slots, part_slots)
        return pltpu.make_async_copy(in_hbm.at[at], arrived.at[at], in_sem.at[q])

    def load_base(c):
        return pltpu.make_async_copy(base_hbm.at[c], base.at[c], base_sem.at[c])

    def store(c, k):
        at = pl.ds(k * cut_rows, cut_rows)
        return pltpu.make_async_copy(out.at[c, at], out_hbm.at[c, at], out_sem.at[c, k])

    for q in range(parts):
        load(q).start()
    for c in range(channels):
        load_base(c).start()
    for q in range(parts):
        load(q).wait()

        def place(j, q=q):
            slot = q * part_slots + j
            at = pl.ds(pl.multiple_of(table_ref[0, slot] * TROWS, TROWS), TROWS)
            rows_back[at, :] = arrived[slot].astype(jnp.float32)

        loop(part_slots, place, unroll=16)
    for c in range(channels):
        size = size_ref[c]
        load_base(c).wait()
        for k in range(cuts):

            def block(b, c=c, k=k, size=size):
                first = pl.multiple_of(k * cut_rows + b * ROWS, ROWS)
                rows = pl.ds(first, ROWS)
                start = (c * extent + first) * panels
                inside = inside_of(first, ROWS, extent, size)
                for p in range(panels):
                    lanes = slice(p * LANES, (p + 1) * LANES)
                    back = rows_back[pl.ds(start + p, ROWS, stride=panels), :]
                    total = base[c, rows, lanes] + flow_step * back
                    out[c, rows, lanes] = jnp.where(inside[:, lanes], total, 0.0)

            loop(cut_rows // ROWS, block, unroll=2)
            store(c, k).start()
    for c in range(channels):
        for k in range(cuts):
            store(c, k).wait()


ANY = functools.partial(pl.BlockSpec, memory_space=pl.ANY)
SMEM = functools.partial(pl.BlockSpec, memory_space=pltpu.SMEM)
WHOLE = functools.partial(pl.BlockSpec, memory_space=pltpu.VMEM)


def per_device(
    generator, hamiltonian, pair_weight, cross_weight, channel_size, send_table, receive_table
):
    channels, extent, _ = generator.shape
    slots = send_table.shape[1]
    tile_count = channels * extent * extent // (TILE * TILE)
    lane_rows = (tile_count + 1) * TROWS
    parts = 8
    devices = lax.axis_size(AXES)
    f32, bf16 = jnp.float32, jnp.bfloat16

    outgoing = pl.pallas_call(
        pack_kernel,
        out_shape=jax.ShapeDtypeStruct((slots, 2 * TROWS, LANES), bf16),
        in_specs=[SMEM(), SMEM(), ANY(), ANY()],
        out_specs=ANY(),
        scratch_shapes=[
            pltpu.VMEM((channels, extent, extent), bf16),
            pltpu.VMEM((channels, extent, extent), bf16),
            pltpu.VMEM((lane_rows, LANES), f32),
            pltpu.VMEM((lane_rows, LANES), f32),
            pltpu.VMEM((slots, 2 * TROWS, LANES), bf16),
            pltpu.SemaphoreType.DMA((2, 2 * channels)),
            pltpu.SemaphoreType.DMA((parts,)),
        ],
        compiler_params=params(),
        name="pack",
    )(channel_size, send_table, generator, hamiltonian)

    def exchange(tiles):
        swapped = lax.all_to_all(
            tiles.reshape(devices, slots // devices, *tiles.shape[1:]),
            AXES,
            split_axis=0,
            concat_axis=0,
            tiled=True,
        )
        return swapped.reshape(tiles.shape)

    arrived = exchange(outgoing)

    base = pl.pallas_call(
        ladder_kernel,
        grid=(channels,),
        out_shape=jax.ShapeDtypeStruct((channels, extent, extent), f32),
        in_specs=[
            SMEM(),
            pl.BlockSpec((1, 1, extent), lambda c: (c, 0, 0)),
            pl.BlockSpec((1, extent, extent), lambda c: (c, 0, 0)),
            pl.BlockSpec((1, extent, extent), lambda c: (c, 0, 0)),
        ],
        out_specs=pl.BlockSpec((1, extent, extent), lambda c: (c, 0, 0)),
        scratch_shapes=[pltpu.VMEM((extent, extent), bf16)] * 4
        + [pltpu.VMEM((extent, LANES), f32)],
        compiler_params=params(),
        name="ladder",
    )(channel_size, pair_weight[:, None, :], generator, hamiltonian)

    going_back = pl.pallas_call(
        cross_kernel,
        out_shape=jax.ShapeDtypeStruct((slots, TROWS, LANES), bf16),
        in_specs=[SMEM(), WHOLE(), ANY()],
        out_specs=ANY(),
        scratch_shapes=[
            pltpu.VMEM((slots, 2 * TROWS, LANES), bf16),
            pltpu.VMEM((lane_rows, LANES), f32),
            pltpu.VMEM((lane_rows, LANES), f32),
        ]
        + [pltpu.VMEM((extent, extent), bf16)] * 4
        + [
            pltpu.VMEM((channels, extent, LANES), f32),
            pltpu.VMEM((lane_rows, LANES), f32),
            pltpu.VMEM((slots, TROWS, LANES), bf16),
            pltpu.SemaphoreType.DMA((parts,)),
            pltpu.SemaphoreType.DMA((parts,)),
        ],
        compiler_params=params(),
        name="cross",
    )(receive_table, cross_weight, arrived)

    came_back = exchange(going_back)

    return pl.pallas_call(
        finish_kernel,
        out_shape=jax.ShapeDtypeStruct((channels, extent, extent), f32),
        in_specs=[SMEM(), SMEM(), ANY(), ANY()],
        out_specs=ANY(),
        scratch_shapes=[
            pltpu.VMEM((channels, extent, extent), f32),
            pltpu.VMEM((slots, TROWS, LANES), bf16),
            pltpu.VMEM((lane_rows, LANES), f32),
            pltpu.VMEM((channels, extent, extent), f32),
            pltpu.SemaphoreType.DMA((channels,)),
            pltpu.SemaphoreType.DMA((parts,)),
            pltpu.SemaphoreType.DMA((channels, 4)),
        ],
        compiler_params=params(),
        name="finish",
    )(channel_size, send_table, base, came_back)


def solution(mesh):
    in_specs = (
        P(AXES, None, None),
        P(AXES, None, None),
        P(AXES, None),
        P(AXES, None),
        P(AXES),
        P(AXES, None),
        P(AXES, None),
    )
    out_specs = P(AXES, None, None)
    return jax.shard_map(
        per_device, mesh=mesh, in_specs=in_specs, out_specs=out_specs, check_vma=False
    )
```

```python
import functools

import jax
import jax.numpy as jnp
from jax import lax
from jax.experimental import pallas as pl
from jax.experimental.pallas import tpu as pltpu
from jax.sharding import PartitionSpec as P

TILE = 32
LANES = 128
TROWS = TILE * TILE // LANES
ROWS = 16
SLOTS = 16
PAIRS_A_TURN = 13
HALF_WORD = 16

flow_step = 0.5

AXES = ("group", "chan")


def params(mebibytes):
    return pltpu.CompilerParams(vmem_limit_bytes=mebibytes * 1024 * 1024)


def chunks_of(total, count):
    while total % count:
        count -= 1
    return count, total // count


def loop(count, body, unroll=1):
    lax.fori_loop(0, count, lambda i, _: (body(i), 0)[1], 0, unroll=unroll)


def inside_of(first_row, rows, columns, size):
    row = lax.broadcasted_iota(jnp.int32, (rows, columns), 0) + first_row
    column = lax.broadcasted_iota(jnp.int32, (rows, columns), 1)
    return (row < size) & (column < size)


def spread(weight_row, out_ref):
    extent = weight_row.shape[1]
    for k in range(extent // LANES):
        piece = weight_row[:, k * LANES : (k + 1) * LANES]
        out_ref[k * LANES : (k + 1) * LANES, :] = jnp.transpose(
            jnp.broadcast_to(piece, (LANES, LANES))
        )


def pack_kernel(size_hbm, table_hbm, gen_hbm, ham_hbm, out_hbm, size_ref, table_ref, gen, ham, rows, out, small_sem, in_sem, out_sem):
    channels, extent, _ = gen.shape
    slots = out.shape[0]
    panels = extent // LANES
    half = rows.shape[0] // 2
    parts, part_rows = chunks_of(extent, 2)
    out_parts = out_sem.shape[0]
    out_slots = slots // out_parts

    sizes = pltpu.make_async_copy(size_hbm, size_ref, small_sem.at[0])
    table = pltpu.make_async_copy(table_hbm, table_ref, small_sem.at[1])
    sizes.start()

    def loads(c, h):
        at = pl.ds(h * part_rows, part_rows)
        k = c * parts + h
        return (
            pltpu.make_async_copy(gen_hbm.at[c, at], gen.at[c, at], in_sem.at[0, k]),
            pltpu.make_async_copy(ham_hbm.at[c, at], ham.at[c, at], in_sem.at[1, k]),
        )

    for c in range(channels):
        for h in range(parts):
            for copy in loads(c, h):
                copy.start()
    table.start()
    sizes.wait()
    for c in range(channels):
        size = size_ref[c]
        for h in range(parts):
            for copy in loads(c, h):
                copy.wait()

            def block(b, c=c, h=h, size=size):
                first = pl.multiple_of(h * part_rows + b * ROWS, ROWS)
                inside = inside_of(first, ROWS, extent, size)
                base = (c * extent + first) * panels
                for source, offset in ((gen, 0), (ham, half)):
                    values = source[c, pl.ds(first, ROWS), :].astype(jnp.float32)
                    values = jnp.where(inside, values, 0.0)
                    for p in range(panels):
                        rows[pl.ds(base + (offset + p), ROWS, stride=panels), :] = values[
                            :, p * LANES : (p + 1) * LANES
                        ]

            loop(part_rows // ROWS, block, unroll=2)
    table.wait()

    def store(q):
        at = pl.ds(q * out_slots, out_slots)
        return pltpu.make_async_copy(out.at[at], out_hbm.at[at], out_sem.at[q])

    for q in range(out_parts):

        def pick(i, q=q):
            first_slot = q * out_slots + i * SLOTS
            for u in range(SLOTS):
                first = pl.multiple_of(table_ref[0, first_slot + u] * TROWS, TROWS)
                g = rows[pl.ds(first, TROWS), :]
                h = rows[pl.ds(first + half, TROWS), :]
                out[first_slot + u] = jnp.concatenate([g, h], axis=0).astype(jnp.bfloat16)

        loop(out_slots // SLOTS, pick)
        store(q).start()
    for q in range(out_parts):
        store(q).wait()


def rows_kernel(send_ref, receive_ref, send_rows, receive_rows):
    pairs = send_rows.shape[1]

    def one(i):
        for table, packed in ((send_ref, send_rows), (receive_ref, receive_rows)):
            low = table[0, i] * TROWS
            packed[0, i] = low + table[0, i + pairs] * (TROWS << HALF_WORD)

    loop(pairs, one, unroll=8)


def each_slot(packed, start, count, body):
    pairs = packed.shape[1]

    def several(i):
        for u in range(PAIRS_A_TURN):
            slot = start + i * PAIRS_A_TURN + u
            word = packed[0, slot]
            low = pl.multiple_of(word & ((1 << HALF_WORD) - 1), TROWS)
            high = pl.multiple_of(lax.shift_right_logical(word, HALF_WORD), TROWS)
            body(slot, low)
            body(slot + pairs, high)

    loop(count // PAIRS_A_TURN, several)


def paired_copies(source, target, sem, q):
    half = source.shape[0] // 2
    part = half // sem.shape[1]
    copies = []
    for k in range(2):
        at = pl.ds(k * half + q * part, part)
        copies.append(pltpu.make_async_copy(source.at[at], target.at[at], sem.at[k, q]))
    return copies


def cross_kernel(packed, weight_ref, in_hbm, out_hbm, arrived, both_rows, gen, ham, wgen, wham, spread_weight, crossed_rows, out, in_sem, out_sem):
    channels, extent = weight_ref.shape
    panels = extent // LANES
    other = both_rows.shape[0] // 2
    parts = in_sem.shape[1]
    part_pairs = packed.shape[1] // parts

    def place(slot, row):
        both = arrived[slot].astype(jnp.float32)
        both_rows[pl.ds(row, TROWS), :] = both[:TROWS]
        both_rows[pl.ds(row + other, TROWS), :] = both[TROWS:]

    def give(slot, row):
        out[slot] = crossed_rows[pl.ds(row, TROWS), :].astype(jnp.bfloat16)

    for q in range(parts):
        for copy in paired_copies(in_hbm, arrived, in_sem, q):
            copy.start()
    for c in range(channels):
        spread(weight_ref[c : c + 1, :], spread_weight.at[c])
    for q in range(parts):
        for copy in paired_copies(in_hbm, arrived, in_sem, q):
            copy.wait()
        each_slot(packed, q * part_pairs, part_pairs, place)
    for c in range(channels):

        def block(b, c=c):
            first = pl.multiple_of(b * ROWS, ROWS)
            rows = pl.ds(first, ROWS)
            base = (c * extent + first) * panels
            weight = spread_weight[c, rows, :]
            for p in range(0, panels, 2):
                lanes = slice(p * LANES, (p + 2) * LANES)
                g = [both_rows[pl.ds(base + (p + i), ROWS, stride=panels), :] for i in range(2)]
                h = [
                    both_rows[pl.ds(base + (other + p + i), ROWS, stride=panels), :]
                    for i in range(2)
                ]
                for target, pair in (
                    (gen, g),
                    (ham, h),
                    (wgen, [weight * x for x in g]),
                    (wham, [weight * x for x in h]),
                ):
                    target[rows, lanes] = jnp.concatenate(pair, axis=1).astype(jnp.bfloat16)

        loop(extent // ROWS, block, unroll=2)
        step = 2 * LANES
        for n in range(extent // step):
            columns = slice(n * step, (n + 1) * step)
            first = jnp.dot(gen[...], wham[:, columns], preferred_element_type=jnp.float32)
            second = jnp.dot(ham[...], wgen[:, columns], preferred_element_type=jnp.float32)
            product = first - second
            for i in range(step // LANES):
                p = n * (step // LANES) + i
                crossed_rows[
                    pl.ds(c * extent * panels + p, extent, stride=panels), :
                ] = product[:, i * LANES : (i + 1) * LANES]

    for q in range(parts):
        each_slot(packed, q * part_pairs, part_pairs, give)
        for copy in paired_copies(out, out_hbm, out_sem, q):
            copy.start()
    for q in range(parts):
        for copy in paired_copies(out, out_hbm, out_sem, q):
            copy.wait()


def ladder_kernel(size_ref, weight_ref, gen_ref, ham_ref, out_ref, gen, ham, wgen, wham, spread_weight):
    channels, extent, _ = gen_ref.shape
    for c in range(channels):
        size = size_ref[c]
        spread(weight_ref[c : c + 1, :], spread_weight)

        def block(b, c=c, size=size):
            rows = pl.ds(pl.multiple_of(b * ROWS, ROWS), ROWS)
            inside = inside_of(b * ROWS, ROWS, extent, size)
            weight = jnp.tile(spread_weight[rows, :], (1, extent // LANES))
            g = jnp.where(inside, gen_ref[c, rows, :].astype(jnp.float32), 0.0)
            h = jnp.where(inside, ham_ref[c, rows, :].astype(jnp.float32), 0.0)
            gen[rows, :] = g.astype(jnp.bfloat16)
            ham[rows, :] = h.astype(jnp.bfloat16)
            wgen[rows, :] = (weight * g).astype(jnp.bfloat16)
            wham[rows, :] = (weight * h).astype(jnp.bfloat16)

        loop(extent // ROWS, block)
        step = 2 * LANES
        for n in range(extent // step):
            columns = slice(n * step, (n + 1) * step)
            first = jnp.dot(gen[...], wham[:, columns], preferred_element_type=jnp.float32)
            second = jnp.dot(ham[...], wgen[:, columns], preferred_element_type=jnp.float32)
            out_ref[c, :, columns] = ham[:, columns].astype(jnp.float32) + flow_step * (
                first - second
            )


def finish_kernel(size_ref, packed, base_hbm, in_hbm, out_hbm, base, arrived, back_rows, out, base_sem, in_sem, out_sem):
    channels, extent, _ = base.shape
    panels = extent // LANES
    parts = in_sem.shape[1]
    part_pairs = packed.shape[1] // parts
    cuts = out_sem.shape[1]
    cut_rows = extent // cuts

    def load_base(c):
        return pltpu.make_async_copy(base_hbm.at[c], base.at[c], base_sem.at[c])

    def store(c, k):
        at = pl.ds(k * cut_rows, cut_rows)
        return pltpu.make_async_copy(out.at[c, at], out_hbm.at[c, at], out_sem.at[c, k])

    def place(slot, row):
        back_rows[pl.ds(row, TROWS), :] = arrived[slot].astype(jnp.float32)

    for q in range(parts):
        for copy in paired_copies(in_hbm, arrived, in_sem, q):
            copy.start()
    for c in range(channels):
        load_base(c).start()
    for q in range(parts):
        for copy in paired_copies(in_hbm, arrived, in_sem, q):
            copy.wait()
        each_slot(packed, q * part_pairs, part_pairs, place)
    for c in range(channels):
        size = size_ref[c]
        load_base(c).wait()
        for k in range(cuts):

            def block(b, c=c, k=k, size=size):
                first = pl.multiple_of(k * cut_rows + b * ROWS, ROWS)
                rows = pl.ds(first, ROWS)
                start = (c * extent + first) * panels
                inside = inside_of(first, ROWS, extent, size)
                for p in range(panels):
                    lanes = slice(p * LANES, (p + 1) * LANES)
                    back = back_rows[pl.ds(start + p, ROWS, stride=panels), :]
                    total = base[c, rows, lanes] + flow_step * back
                    out[c, rows, lanes] = jnp.where(inside[:, lanes], total, 0.0)

            loop(cut_rows // ROWS, block, unroll=2)
            store(c, k).start()
    for c in range(channels):
        for k in range(cuts):
            store(c, k).wait()


HBM = functools.partial(pl.BlockSpec, memory_space=pltpu.HBM)
SMEM = functools.partial(pl.BlockSpec, memory_space=pltpu.SMEM)
WHOLE = functools.partial(pl.BlockSpec, memory_space=pltpu.VMEM)


def per_device(
    generator, hamiltonian, pair_weight, cross_weight, channel_size, send_table, receive_table
):
    channels, extent, _ = generator.shape
    slots = send_table.shape[1]
    panels = extent // LANES
    lane_rows = channels * extent * panels + TROWS
    parts = 8
    devices = lax.axis_size(AXES)
    f32, bf16 = jnp.float32, jnp.bfloat16

    outgoing = pl.pallas_call(
        pack_kernel,
        out_shape=jax.ShapeDtypeStruct((slots, 2 * TROWS, LANES), bf16),
        in_specs=[HBM()] * 4,
        out_specs=HBM(),
        scratch_shapes=[
            pltpu.SMEM(channel_size.shape, jnp.int32),
            pltpu.SMEM(send_table.shape, jnp.int32),
            pltpu.VMEM((channels, extent, extent), bf16),
            pltpu.VMEM((channels, extent, extent), bf16),
            pltpu.VMEM((2 * lane_rows, LANES), f32),
            pltpu.VMEM((slots, 2 * TROWS, LANES), bf16),
            pltpu.SemaphoreType.DMA((2,)),
            pltpu.SemaphoreType.DMA((2, 2 * channels)),
            pltpu.SemaphoreType.DMA((parts,)),
        ],
        compiler_params=params(60),
        name="pack",
    )(channel_size, send_table, generator, hamiltonian)

    def exchange(tiles):
        swapped = lax.all_to_all(
            tiles.reshape(devices, slots // devices, *tiles.shape[1:]),
            AXES,
            split_axis=0,
            concat_axis=0,
            tiled=True,
        )
        return swapped.reshape(tiles.shape)

    arrived = exchange(outgoing)

    send_rows, receive_rows = pl.pallas_call(
        rows_kernel,
        out_shape=[jax.ShapeDtypeStruct((1, slots // 2), jnp.int32)] * 2,
        in_specs=[SMEM(), SMEM()],
        out_specs=[SMEM(), SMEM()],
        compiler_params=params(2),
        name="rows",
    )(send_table, receive_table)

    base = pl.pallas_call(
        ladder_kernel,
        out_shape=jax.ShapeDtypeStruct((channels, extent, extent), f32),
        in_specs=[SMEM(), WHOLE(), WHOLE(), WHOLE()],
        out_specs=WHOLE(),
        scratch_shapes=[pltpu.VMEM((extent, extent), bf16)] * 4
        + [pltpu.VMEM((extent, LANES), f32)],
        compiler_params=params(20),
        name="ladder",
    )(channel_size, pair_weight, generator, hamiltonian)

    going_back = pl.pallas_call(
        cross_kernel,
        out_shape=jax.ShapeDtypeStruct((slots, TROWS, LANES), bf16),
        in_specs=[SMEM(), WHOLE(), HBM()],
        out_specs=HBM(),
        scratch_shapes=[
            pltpu.VMEM((slots, 2 * TROWS, LANES), bf16),
            pltpu.VMEM((2 * lane_rows, LANES), f32),
        ]
        + [pltpu.VMEM((extent, extent), bf16)] * 4
        + [
            pltpu.VMEM((channels, extent, LANES), f32),
            pltpu.VMEM((lane_rows, LANES), f32),
            pltpu.VMEM((slots, TROWS, LANES), bf16),
            pltpu.SemaphoreType.DMA((2, parts)),
            pltpu.SemaphoreType.DMA((2, parts)),
        ],
        compiler_params=params(60),
        name="cross",
    )(receive_rows, cross_weight, arrived)

    came_back = exchange(going_back)

    return pl.pallas_call(
        finish_kernel,
        out_shape=jax.ShapeDtypeStruct((channels, extent, extent), f32),
        in_specs=[SMEM(), SMEM(), HBM(), HBM()],
        out_specs=HBM(),
        scratch_shapes=[
            pltpu.VMEM((channels, extent, extent), f32),
            pltpu.VMEM((slots, TROWS, LANES), bf16),
            pltpu.VMEM((lane_rows, LANES), f32),
            pltpu.VMEM((channels, extent, extent), f32),
            pltpu.SemaphoreType.DMA((channels,)),
            pltpu.SemaphoreType.DMA((2, parts)),
            pltpu.SemaphoreType.DMA((channels, 4)),
        ],
        compiler_params=params(60),
        name="finish",
    )(channel_size, send_rows, base, came_back)


def solution(mesh):
    in_specs = (
        P(AXES, None, None),
        P(AXES, None, None),
        P(AXES, None),
        P(AXES, None),
        P(AXES),
        P(AXES, None),
        P(AXES, None),
    )
    out_specs = P(AXES, None, None)
    return jax.shard_map(
        per_device, mesh=mesh, in_specs=in_specs, out_specs=out_specs, check_vma=False
    )
```

```python
import functools

import jax
import jax.numpy as jnp
from jax import lax
from jax.experimental import pallas as pl
from jax.experimental.pallas import tpu as pltpu
from jax.sharding import PartitionSpec as P

TILE = 32
LANES = 128
TROWS = TILE * TILE // LANES
ROWS = 16

flow_step = 0.5

PACK_MIB, LADDER_MIB, CROSS_MIB, FINISH_MIB = 60, 20, 40, 50

AXES = ("group", "chan")
X_BITS, Y_BITS, Z_BITS, CORE_BITS = 2, 2, 2, 1
DEVICES = 1 << (X_BITS + Y_BITS + Z_BITS + CORE_BITS)


def device_at(place):
    x = place & ((1 << X_BITS) - 1)
    place = place >> X_BITS
    z = place & ((1 << Z_BITS) - 1)
    place = place >> Z_BITS
    core = place & ((1 << CORE_BITS) - 1)
    y = place >> CORE_BITS
    return (((((x << Y_BITS) | y) << Z_BITS) | z) << CORE_BITS) | core


ORDER = [device_at(place) for place in range(DEVICES)]


def params(mebibytes):
    return pltpu.CompilerParams(vmem_limit_bytes=mebibytes * 1024 * 1024)


def chunks_of(total, count):
    while total % count:
        count -= 1
    return count, total // count


def loop(count, body, unroll=1):
    lax.fori_loop(0, count, lambda i, _: (body(i), 0)[1], 0, unroll=unroll)


def inside_of(first_row, rows, columns, size):
    row = lax.broadcasted_iota(jnp.int32, (rows, columns), 0) + first_row
    column = lax.broadcasted_iota(jnp.int32, (rows, columns), 1)
    return (row < size) & (column < size)


def spread(weight_row, out_ref):
    extent = weight_row.shape[1]
    for k in range(extent // LANES):
        piece = weight_row[:, k * LANES : (k + 1) * LANES]
        out_ref[k * LANES : (k + 1) * LANES, :] = jnp.transpose(
            jnp.broadcast_to(piece, (LANES, LANES))
        )


def pack_kernel(size_hbm, table_hbm, gen_hbm, ham_hbm, out_hbm, size_ref, table, words, first_rows, gen, ham, rows, out, small_sem, in_sem, out_sem):
    channels, extent, _ = gen.shape
    panels = extent // LANES
    half = rows.shape[0] // 2
    parts, part_rows = chunks_of(extent, 2)
    capacity = first_rows.shape[1] // DEVICES
    out_parts = out_sem.shape[0]
    out_places = DEVICES // out_parts

    read_table = pltpu.make_async_copy(table_hbm, table, small_sem.at[0])
    read_sizes = pltpu.make_async_copy(size_hbm, size_ref, small_sem.at[1])
    give_rows = pltpu.make_async_copy(words, first_rows, small_sem.at[2])
    read_table.start()
    read_sizes.start()

    def loads(c, h):
        at = pl.ds(h * part_rows, part_rows)
        k = c * parts + h
        return (
            pltpu.make_async_copy(gen_hbm.at[c, at], gen.at[c, at], in_sem.at[0, k]),
            pltpu.make_async_copy(ham_hbm.at[c, at], ham.at[c, at], in_sem.at[1, k]),
        )

    for c in range(channels):
        for h in range(parts):
            for copy in loads(c, h):
                copy.start()
    read_table.wait()
    words[...] = table[...] * TROWS
    give_rows.start()
    read_sizes.wait()
    for c in range(channels):
        size = size_ref[c]
        for h in range(parts):
            for copy in loads(c, h):
                copy.wait()

            def block(b, c=c, h=h, size=size):
                first = pl.multiple_of(h * part_rows + b * ROWS, ROWS)
                inside = inside_of(first, ROWS, extent, size)
                base = (c * extent + first) * panels
                for source, offset in ((gen, 0), (ham, half)):
                    values = source[c, pl.ds(first, ROWS), :].astype(jnp.float32)
                    values = jnp.where(inside, values, 0.0)
                    for p in range(panels):
                        rows[pl.ds(base + (offset + p), ROWS, stride=panels), :] = values[
                            :, p * LANES : (p + 1) * LANES
                        ]

            loop(part_rows // ROWS, block, unroll=2)
    give_rows.wait()

    def store(q):
        at = pl.ds(q * out_places * capacity, out_places * capacity)
        return pltpu.make_async_copy(out.at[at], out_hbm.at[at], out_sem.at[q])

    def pick(slot, row):
        g = rows[pl.ds(row, TROWS), :]
        h = rows[pl.ds(row + half, TROWS), :]
        out[slot] = jnp.concatenate([g, h], axis=0).astype(jnp.bfloat16)

    for q in range(out_parts):
        each_slot(first_rows, q * out_places, out_places, pick)
        store(q).start()
    for q in range(out_parts):
        store(q).wait()


def each_slot(first_rows, start, count, body):
    capacity = first_rows.shape[1] // DEVICES
    for place in range(start, start + count):
        for k in range(capacity):
            row = first_rows[0, ORDER[place] * capacity + k]
            body(place * capacity + k, pl.multiple_of(row, TROWS))


def cross_kernel(table, weight_ref, arrived, out_hbm, words, first_rows, both_rows, gen, ham, wgen, wham, spread_weight, crossed_rows, out, small_sem, out_sem):
    channels, extent = weight_ref.shape
    panels = extent // LANES
    other = both_rows.shape[0] // 2
    parts = out_sem.shape[0]
    part_places = DEVICES // parts
    part_slots = out.shape[0] // parts
    give_rows = pltpu.make_async_copy(words, first_rows, small_sem)

    def place(slot, row):
        both = arrived[slot].astype(jnp.float32)
        both_rows[pl.ds(row, TROWS), :] = both[:TROWS]
        both_rows[pl.ds(row + other, TROWS), :] = both[TROWS:]

    def give(slot, row):
        out[slot] = crossed_rows[pl.ds(row, TROWS), :].astype(jnp.bfloat16)

    def store(q):
        at = pl.ds(q * part_slots, part_slots)
        return pltpu.make_async_copy(out.at[at], out_hbm.at[at], out_sem.at[q])

    words[...] = table[...] * TROWS
    give_rows.start()
    for c in range(channels):
        spread(weight_ref[c : c + 1, :], spread_weight.at[c])
    give_rows.wait()
    each_slot(first_rows, 0, DEVICES, place)
    for c in range(channels):

        def block(b, c=c):
            first = pl.multiple_of(b * ROWS, ROWS)
            rows = pl.ds(first, ROWS)
            base = (c * extent + first) * panels
            weight = spread_weight[c, rows, :]
            for p in range(0, panels, 2):
                lanes = slice(p * LANES, (p + 2) * LANES)
                g = [both_rows[pl.ds(base + (p + i), ROWS, stride=panels), :] for i in range(2)]
                h = [
                    both_rows[pl.ds(base + (other + p + i), ROWS, stride=panels), :]
                    for i in range(2)
                ]
                for target, pair in (
                    (gen, g),
                    (ham, h),
                    (wgen, [weight * x for x in g]),
                    (wham, [weight * x for x in h]),
                ):
                    target[rows, lanes] = jnp.concatenate(pair, axis=1).astype(jnp.bfloat16)

        loop(extent // ROWS, block, unroll=2)
        step = 2 * LANES
        for n in range(extent // step):
            columns = slice(n * step, (n + 1) * step)
            first = jnp.dot(gen[...], wham[:, columns], preferred_element_type=jnp.float32)
            second = jnp.dot(ham[...], wgen[:, columns], preferred_element_type=jnp.float32)
            product = first - second
            for i in range(step // LANES):
                p = n * (step // LANES) + i
                crossed_rows[
                    pl.ds(c * extent * panels + p, extent, stride=panels), :
                ] = product[:, i * LANES : (i + 1) * LANES]

    for q in range(parts):
        each_slot(first_rows, q * part_places, part_places, give)
        store(q).start()
    for q in range(parts):
        store(q).wait()


def ladder_kernel(size_ref, weight_ref, gen_ref, ham_ref, out_ref, gen, ham, wgen, wham, spread_weight):
    channels, extent, _ = gen_ref.shape
    for c in range(channels):
        size = size_ref[c]
        spread(weight_ref[c : c + 1, :], spread_weight)

        def block(b, c=c, size=size):
            rows = pl.ds(pl.multiple_of(b * ROWS, ROWS), ROWS)
            inside = inside_of(b * ROWS, ROWS, extent, size)
            weight = jnp.tile(spread_weight[rows, :], (1, extent // LANES))
            g = jnp.where(inside, gen_ref[c, rows, :].astype(jnp.float32), 0.0)
            h = jnp.where(inside, ham_ref[c, rows, :].astype(jnp.float32), 0.0)
            gen[rows, :] = g.astype(jnp.bfloat16)
            ham[rows, :] = h.astype(jnp.bfloat16)
            wgen[rows, :] = (weight * g).astype(jnp.bfloat16)
            wham[rows, :] = (weight * h).astype(jnp.bfloat16)

        loop(extent // ROWS, block)
        step = 2 * LANES
        for n in range(extent // step):
            columns = slice(n * step, (n + 1) * step)
            first = jnp.dot(gen[...], wham[:, columns], preferred_element_type=jnp.float32)
            second = jnp.dot(ham[...], wgen[:, columns], preferred_element_type=jnp.float32)
            out_ref[c, :, columns] = ham[:, columns].astype(jnp.float32) + flow_step * (
                first - second
            )


def finish_kernel(size_hbm, table, base_hbm, arrived, out_hbm, size_ref, words, first_rows, base, back_rows, out, small_sem, base_sem, out_sem):
    channels, extent, _ = base.shape
    panels = extent // LANES
    cuts = out_sem.shape[1]
    cut_rows = extent // cuts
    give_rows = pltpu.make_async_copy(words, first_rows, small_sem.at[0])
    read_sizes = pltpu.make_async_copy(size_hbm, size_ref, small_sem.at[1])

    def load_base(c):
        return pltpu.make_async_copy(base_hbm.at[c], base.at[c], base_sem.at[c])

    def store(c, k):
        at = pl.ds(k * cut_rows, cut_rows)
        return pltpu.make_async_copy(out.at[c, at], out_hbm.at[c, at], out_sem.at[c, k])

    def place(slot, row):
        back_rows[pl.ds(row, TROWS), :] = arrived[slot].astype(jnp.float32)

    words[...] = table[...] * TROWS
    give_rows.start()
    read_sizes.start()
    for c in range(channels):
        load_base(c).start()
    give_rows.wait()
    each_slot(first_rows, 0, DEVICES, place)
    read_sizes.wait()
    for c in range(channels):
        size = size_ref[c]
        load_base(c).wait()
        for k in range(cuts):

            def block(b, c=c, k=k, size=size):
                first = pl.multiple_of(k * cut_rows + b * ROWS, ROWS)
                rows = pl.ds(first, ROWS)
                start = (c * extent + first) * panels
                inside = inside_of(first, ROWS, extent, size)
                for p in range(panels):
                    lanes = slice(p * LANES, (p + 1) * LANES)
                    back = back_rows[pl.ds(start + p, ROWS, stride=panels), :]
                    total = base[c, rows, lanes] + flow_step * back
                    out[c, rows, lanes] = jnp.where(inside[:, lanes], total, 0.0)

            loop(cut_rows // ROWS, block, unroll=2)
            store(c, k).start()
    for c in range(channels):
        for k in range(cuts):
            store(c, k).wait()


HBM = functools.partial(pl.BlockSpec, memory_space=pltpu.HBM)
SMEM = functools.partial(pl.BlockSpec, memory_space=pltpu.SMEM)
WHOLE = functools.partial(pl.BlockSpec, memory_space=pltpu.VMEM)


def per_device(
    generator, hamiltonian, pair_weight, cross_weight, channel_size, send_table, receive_table
):
    channels, extent, _ = generator.shape
    slots = send_table.shape[1]
    panels = extent // LANES
    lane_rows = channels * extent * panels + TROWS
    parts = 8
    devices = lax.axis_size(AXES)
    f32, bf16 = jnp.float32, jnp.bfloat16

    outgoing = pl.pallas_call(
        pack_kernel,
        out_shape=jax.ShapeDtypeStruct((slots, 2 * TROWS, LANES), bf16),
        in_specs=[HBM()] * 4,
        out_specs=HBM(),
        scratch_shapes=[
            pltpu.SMEM(channel_size.shape, jnp.int32),
            pltpu.VMEM(send_table.shape, jnp.int32),
            pltpu.VMEM((1, slots), jnp.int32),
            pltpu.SMEM((1, slots), jnp.int32),
            pltpu.VMEM((channels, extent, extent), bf16),
            pltpu.VMEM((channels, extent, extent), bf16),
            pltpu.VMEM((2 * lane_rows, LANES), f32),
            pltpu.VMEM((slots, 2 * TROWS, LANES), bf16),
            pltpu.SemaphoreType.DMA((3,)),
            pltpu.SemaphoreType.DMA((2, 2 * channels)),
            pltpu.SemaphoreType.DMA((parts,)),
        ],
        compiler_params=params(PACK_MIB),
        name="pack",
    )(channel_size, send_table, generator, hamiltonian)

    def exchange(tiles):
        swapped = lax.all_to_all(
            tiles.reshape(devices, slots // devices, *tiles.shape[1:]),
            AXES,
            split_axis=0,
            concat_axis=0,
            tiled=True,
            axis_index_groups=[ORDER],
        )
        return swapped.reshape(tiles.shape)

    arrived = exchange(outgoing)

    base = pl.pallas_call(
        ladder_kernel,
        out_shape=jax.ShapeDtypeStruct((channels, extent, extent), f32),
        in_specs=[SMEM(), WHOLE(), WHOLE(), WHOLE()],
        out_specs=WHOLE(),
        scratch_shapes=[pltpu.VMEM((extent, extent), bf16)] * 4
        + [pltpu.VMEM((extent, LANES), f32)],
        compiler_params=params(LADDER_MIB),
        name="ladder",
    )(channel_size, pair_weight, generator, hamiltonian)

    table_words = [
        pltpu.VMEM((1, slots), jnp.int32),
        pltpu.SMEM((1, slots), jnp.int32),
    ]
    going_back = pl.pallas_call(
        cross_kernel,
        out_shape=jax.ShapeDtypeStruct((slots, TROWS, LANES), bf16),
        in_specs=[WHOLE(), WHOLE(), WHOLE()],
        out_specs=HBM(),
        scratch_shapes=table_words
        + [pltpu.VMEM((2 * lane_rows, LANES), f32)]
        + [pltpu.VMEM((extent, extent), bf16)] * 4
        + [
            pltpu.VMEM((channels, extent, LANES), f32),
            pltpu.VMEM((lane_rows, LANES), f32),
            pltpu.VMEM((slots, TROWS, LANES), bf16),
            pltpu.SemaphoreType.DMA,
            pltpu.SemaphoreType.DMA((parts,)),
        ],
        compiler_params=params(CROSS_MIB),
        name="cross",
    )(receive_table, cross_weight, arrived)

    came_back = exchange(going_back)

    return pl.pallas_call(
        finish_kernel,
        out_shape=jax.ShapeDtypeStruct((channels, extent, extent), f32),
        in_specs=[HBM(), WHOLE(), HBM(), WHOLE()],
        out_specs=HBM(),
        scratch_shapes=[pltpu.SMEM(channel_size.shape, jnp.int32)]
        + table_words
        + [
            pltpu.VMEM((channels, extent, extent), f32),
            pltpu.VMEM((lane_rows, LANES), f32),
            pltpu.VMEM((channels, extent, extent), f32),
            pltpu.SemaphoreType.DMA((2,)),
            pltpu.SemaphoreType.DMA((channels,)),
            pltpu.SemaphoreType.DMA((channels, 4)),
        ],
        compiler_params=params(FINISH_MIB),
        name="finish",
    )(channel_size, send_table, base, came_back)


def solution(mesh):
    in_specs = (
        P(AXES, None, None),
        P(AXES, None, None),
        P(AXES, None),
        P(AXES, None),
        P(AXES),
        P(AXES, None),
        P(AXES, None),
    )
    out_specs = P(AXES, None, None)
    return jax.shard_map(
        per_device, mesh=mesh, in_specs=in_specs, out_specs=out_specs, check_vma=False
    )
```

```python
import functools

import jax
import jax.numpy as jnp
from jax import lax
from jax.experimental import pallas as pl
from jax.experimental.pallas import tpu as pltpu
from jax.sharding import PartitionSpec as P

TILE = 32
LANES = 128
TROWS = TILE * TILE // LANES
ROWS = 16

flow_step = 0.5

PACK_MIB, LADDER_MIB, CROSS_MIB, FINISH_MIB = 40, 20, 40, 50

AXES = ("group", "chan")
X_BITS, Y_BITS, Z_BITS, CORE_BITS = 2, 2, 2, 1
DEVICES = 1 << (X_BITS + Y_BITS + Z_BITS + CORE_BITS)


def device_at(place):
    x = place & ((1 << X_BITS) - 1)
    place = place >> X_BITS
    z = place & ((1 << Z_BITS) - 1)
    place = place >> Z_BITS
    core = place & ((1 << CORE_BITS) - 1)
    y = place >> CORE_BITS
    return (((((x << Y_BITS) | y) << Z_BITS) | z) << CORE_BITS) | core


ORDER = [device_at(place) for place in range(DEVICES)]


def params(mebibytes):
    return pltpu.CompilerParams(vmem_limit_bytes=mebibytes * 1024 * 1024)


def chunks_of(total, count):
    while total % count:
        count -= 1
    return count, total // count


def loop(count, body, unroll=1):
    lax.fori_loop(0, count, lambda i, _: (body(i), 0)[1], 0, unroll=unroll)


def inside_of(first_row, rows, columns, size):
    row = lax.broadcasted_iota(jnp.int32, (rows, columns), 0) + first_row
    column = lax.broadcasted_iota(jnp.int32, (rows, columns), 1)
    return (row < size) & (column < size)


def spread(weight_row, out_ref):
    extent = weight_row.shape[1]
    for k in range(extent // LANES):
        piece = weight_row[:, k * LANES : (k + 1) * LANES]
        out_ref[k * LANES : (k + 1) * LANES, :] = jnp.transpose(
            jnp.broadcast_to(piece, (LANES, LANES))
        )


def pack_kernel(size_hbm, table_hbm, gen_hbm, ham_hbm, out, size_ref, table, words, first_rows, gen, ham, rows, small_sem, in_sem):
    channels, extent, _ = gen.shape
    panels = extent // LANES
    half = rows.shape[0] // 2
    parts, part_rows = chunks_of(extent, 2)
    read_table = pltpu.make_async_copy(table_hbm, table, small_sem.at[0])
    read_sizes = pltpu.make_async_copy(size_hbm, size_ref, small_sem.at[1])
    give_rows = pltpu.make_async_copy(words, first_rows, small_sem.at[2])
    read_table.start()
    read_sizes.start()

    def loads(c, h):
        at = pl.ds(h * part_rows, part_rows)
        k = c * parts + h
        return (
            pltpu.make_async_copy(gen_hbm.at[c, at], gen.at[c, at], in_sem.at[0, k]),
            pltpu.make_async_copy(ham_hbm.at[c, at], ham.at[c, at], in_sem.at[1, k]),
        )

    for c in range(channels):
        for h in range(parts):
            for copy in loads(c, h):
                copy.start()
    read_table.wait()
    words[...] = table[...] * TROWS
    give_rows.start()
    read_sizes.wait()
    for c in range(channels):
        size = size_ref[c]
        for h in range(parts):
            for copy in loads(c, h):
                copy.wait()

            def block(b, c=c, h=h, size=size):
                first = pl.multiple_of(h * part_rows + b * ROWS, ROWS)
                inside = inside_of(first, ROWS, extent, size)
                base = (c * extent + first) * panels
                for source, offset in ((gen, 0), (ham, half)):
                    values = source[c, pl.ds(first, ROWS), :].astype(jnp.float32)
                    values = jnp.where(inside, values, 0.0)
                    for p in range(panels):
                        rows[pl.ds(base + (offset + p), ROWS, stride=panels), :] = values[
                            :, p * LANES : (p + 1) * LANES
                        ]

            loop(part_rows // ROWS, block, unroll=2)
    give_rows.wait()

    def pick(slot, row):
        g = rows[pl.ds(row, TROWS), :]
        h = rows[pl.ds(row + half, TROWS), :]
        out[slot] = jnp.concatenate([g, h], axis=0).astype(jnp.bfloat16)

    each_slot(first_rows, 0, DEVICES, pick)


def each_slot(first_rows, start, count, body):
    capacity = first_rows.shape[1] // DEVICES
    for place in range(start, start + count):
        for k in range(capacity):
            row = first_rows[0, ORDER[place] * capacity + k]
            body(place * capacity + k, pl.multiple_of(row, TROWS))


def cross_kernel(table, weight_ref, arrived, out_hbm, words, first_rows, both_rows, gen, ham, wgen, wham, spread_weight, crossed_rows, out, small_sem, out_sem):
    channels, extent = weight_ref.shape
    panels = extent // LANES
    other = both_rows.shape[0] // 2
    parts = out_sem.shape[0]
    part_places = DEVICES // parts
    part_slots = out.shape[0] // parts
    give_rows = pltpu.make_async_copy(words, first_rows, small_sem)

    def place(slot, row):
        both = arrived[slot].astype(jnp.float32)
        both_rows[pl.ds(row, TROWS), :] = both[:TROWS]
        both_rows[pl.ds(row + other, TROWS), :] = both[TROWS:]

    def give(slot, row):
        out[slot] = crossed_rows[pl.ds(row, TROWS), :].astype(jnp.bfloat16)

    def store(q):
        at = pl.ds(q * part_slots, part_slots)
        return pltpu.make_async_copy(out.at[at], out_hbm.at[at], out_sem.at[q])

    words[...] = table[...] * TROWS
    give_rows.start()
    for c in range(channels):
        spread(weight_ref[c : c + 1, :], spread_weight.at[c])
    give_rows.wait()
    each_slot(first_rows, 0, DEVICES, place)
    for c in range(channels):

        def block(b, c=c):
            first = pl.multiple_of(b * ROWS, ROWS)
            rows = pl.ds(first, ROWS)
            base = (c * extent + first) * panels
            weight = spread_weight[c, rows, :]
            for p in range(0, panels, 2):
                lanes = slice(p * LANES, (p + 2) * LANES)
                g = [both_rows[pl.ds(base + (p + i), ROWS, stride=panels), :] for i in range(2)]
                h = [
                    both_rows[pl.ds(base + (other + p + i), ROWS, stride=panels), :]
                    for i in range(2)
                ]
                for target, pair in (
                    (gen, g),
                    (ham, h),
                    (wgen, [weight * x for x in g]),
                    (wham, [weight * x for x in h]),
                ):
                    target[rows, lanes] = jnp.concatenate(pair, axis=1).astype(jnp.bfloat16)

        loop(extent // ROWS, block, unroll=2)
        step = 2 * LANES
        for n in range(extent // step):
            columns = slice(n * step, (n + 1) * step)
            first = jnp.dot(gen[...], wham[:, columns], preferred_element_type=jnp.float32)
            second = jnp.dot(ham[...], wgen[:, columns], preferred_element_type=jnp.float32)
            product = first - second
            for i in range(step // LANES):
                p = n * (step // LANES) + i
                crossed_rows[
                    pl.ds(c * extent * panels + p, extent, stride=panels), :
                ] = product[:, i * LANES : (i + 1) * LANES]

    for q in range(parts):
        each_slot(first_rows, q * part_places, part_places, give)
        store(q).start()
    for q in range(parts):
        store(q).wait()


def ladder_kernel(size_ref, weight_ref, gen_ref, ham_ref, out_ref, gen, ham, wgen, wham, spread_weight):
    channels, extent, _ = gen_ref.shape
    for c in range(channels):
        size = size_ref[c]
        spread(weight_ref[c : c + 1, :], spread_weight)

        def block(b, c=c, size=size):
            rows = pl.ds(pl.multiple_of(b * ROWS, ROWS), ROWS)
            inside = inside_of(b * ROWS, ROWS, extent, size)
            weight = jnp.tile(spread_weight[rows, :], (1, extent // LANES))
            g = jnp.where(inside, gen_ref[c, rows, :].astype(jnp.float32), 0.0)
            h = jnp.where(inside, ham_ref[c, rows, :].astype(jnp.float32), 0.0)
            gen[rows, :] = g.astype(jnp.bfloat16)
            ham[rows, :] = h.astype(jnp.bfloat16)
            wgen[rows, :] = (weight * g).astype(jnp.bfloat16)
            wham[rows, :] = (weight * h).astype(jnp.bfloat16)

        loop(extent // ROWS, block)
        step = 2 * LANES
        for n in range(extent // step):
            columns = slice(n * step, (n + 1) * step)
            first = jnp.dot(gen[...], wham[:, columns], preferred_element_type=jnp.float32)
            second = jnp.dot(ham[...], wgen[:, columns], preferred_element_type=jnp.float32)
            out_ref[c, :, columns] = ham[:, columns].astype(jnp.float32) + flow_step * (
                first - second
            )


def finish_kernel(size_hbm, table, base_hbm, arrived, out_hbm, size_ref, words, first_rows, base, back_rows, out, small_sem, base_sem, out_sem):
    channels, extent, _ = base.shape
    panels = extent // LANES
    cuts = out_sem.shape[1]
    cut_rows = extent // cuts
    give_rows = pltpu.make_async_copy(words, first_rows, small_sem.at[0])
    read_sizes = pltpu.make_async_copy(size_hbm, size_ref, small_sem.at[1])

    def load_base(c):
        return pltpu.make_async_copy(base_hbm.at[c], base.at[c], base_sem.at[c])

    def store(c, k):
        at = pl.ds(k * cut_rows, cut_rows)
        return pltpu.make_async_copy(out.at[c, at], out_hbm.at[c, at], out_sem.at[c, k])

    def place(slot, row):
        back_rows[pl.ds(row, TROWS), :] = arrived[slot].astype(jnp.float32)

    words[...] = table[...] * TROWS
    give_rows.start()
    read_sizes.start()
    for c in range(channels):
        load_base(c).start()
    give_rows.wait()
    each_slot(first_rows, 0, DEVICES, place)
    read_sizes.wait()
    for c in range(channels):
        size = size_ref[c]
        load_base(c).wait()
        for k in range(cuts):

            def block(b, c=c, k=k, size=size):
                first = pl.multiple_of(k * cut_rows + b * ROWS, ROWS)
                rows = pl.ds(first, ROWS)
                start = (c * extent + first) * panels
                inside = inside_of(first, ROWS, extent, size)
                for p in range(panels):
                    lanes = slice(p * LANES, (p + 1) * LANES)
                    back = back_rows[pl.ds(start + p, ROWS, stride=panels), :]
                    total = base[c, rows, lanes] + flow_step * back
                    out[c, rows, lanes] = jnp.where(inside[:, lanes], total, 0.0)

            loop(cut_rows // ROWS, block, unroll=2)
            store(c, k).start()
    for c in range(channels):
        for k in range(cuts):
            store(c, k).wait()


HBM = functools.partial(pl.BlockSpec, memory_space=pltpu.HBM)
SMEM = functools.partial(pl.BlockSpec, memory_space=pltpu.SMEM)
WHOLE = functools.partial(pl.BlockSpec, memory_space=pltpu.VMEM)


def in_hbm(operand):
    return pltpu.with_memory_space_constraint(operand, pltpu.HBM)


def per_device(
    generator, hamiltonian, pair_weight, cross_weight, channel_size, send_table, receive_table
):
    channels, extent, _ = generator.shape
    slots = send_table.shape[1]
    panels = extent // LANES
    lane_rows = channels * extent * panels + TROWS
    parts = 8
    devices = lax.axis_size(AXES)
    f32, bf16 = jnp.float32, jnp.bfloat16

    outgoing = pl.pallas_call(
        pack_kernel,
        out_shape=jax.ShapeDtypeStruct((slots, 2 * TROWS, LANES), bf16),
        in_specs=[HBM()] * 4,
        out_specs=WHOLE(),
        scratch_shapes=[
            pltpu.SMEM(channel_size.shape, jnp.int32),
            pltpu.VMEM(send_table.shape, jnp.int32),
            pltpu.VMEM((1, slots), jnp.int32),
            pltpu.SMEM((1, slots), jnp.int32),
            pltpu.VMEM((channels, extent, extent), bf16),
            pltpu.VMEM((channels, extent, extent), bf16),
            pltpu.VMEM((2 * lane_rows, LANES), f32),
            pltpu.SemaphoreType.DMA((3,)),
            pltpu.SemaphoreType.DMA((2, 2 * channels)),
        ],
        compiler_params=params(PACK_MIB),
        name="pack",
    )(*(in_hbm(v) for v in (channel_size, send_table, generator, hamiltonian)))

    def exchange(tiles):
        swapped = lax.all_to_all(
            tiles.reshape(devices, slots // devices, *tiles.shape[1:]),
            AXES,
            split_axis=0,
            concat_axis=0,
            tiled=True,
            axis_index_groups=[ORDER],
        )
        return swapped.reshape(tiles.shape)

    arrived = exchange(outgoing)

    base = pl.pallas_call(
        ladder_kernel,
        out_shape=jax.ShapeDtypeStruct((channels, extent, extent), f32),
        in_specs=[SMEM(), WHOLE(), WHOLE(), WHOLE()],
        out_specs=WHOLE(),
        scratch_shapes=[pltpu.VMEM((extent, extent), bf16)] * 4
        + [pltpu.VMEM((extent, LANES), f32)],
        compiler_params=params(LADDER_MIB),
        name="ladder",
    )(channel_size, pair_weight, generator, hamiltonian)

    table_words = [
        pltpu.VMEM((1, slots), jnp.int32),
        pltpu.SMEM((1, slots), jnp.int32),
    ]
    going_back = pl.pallas_call(
        cross_kernel,
        out_shape=jax.ShapeDtypeStruct((slots, TROWS, LANES), bf16),
        in_specs=[WHOLE(), WHOLE(), WHOLE()],
        out_specs=HBM(),
        scratch_shapes=table_words
        + [pltpu.VMEM((2 * lane_rows, LANES), f32)]
        + [pltpu.VMEM((extent, extent), bf16)] * 4
        + [
            pltpu.VMEM((channels, extent, LANES), f32),
            pltpu.VMEM((lane_rows, LANES), f32),
            pltpu.VMEM((slots, TROWS, LANES), bf16),
            pltpu.SemaphoreType.DMA,
            pltpu.SemaphoreType.DMA((parts,)),
        ],
        compiler_params=params(CROSS_MIB),
        name="cross",
    )(receive_table, cross_weight, arrived)

    came_back = exchange(going_back)

    return pl.pallas_call(
        finish_kernel,
        out_shape=jax.ShapeDtypeStruct((channels, extent, extent), f32),
        in_specs=[HBM(), WHOLE(), HBM(), WHOLE()],
        out_specs=HBM(),
        scratch_shapes=[pltpu.SMEM(channel_size.shape, jnp.int32)]
        + table_words
        + [
            pltpu.VMEM((channels, extent, extent), f32),
            pltpu.VMEM((lane_rows, LANES), f32),
            pltpu.VMEM((channels, extent, extent), f32),
            pltpu.SemaphoreType.DMA((2,)),
            pltpu.SemaphoreType.DMA((channels,)),
            pltpu.SemaphoreType.DMA((channels, 4)),
        ],
        compiler_params=params(FINISH_MIB),
        name="finish",
    )(channel_size, send_table, in_hbm(base), came_back)


def solution(mesh):
    in_specs = (
        P(AXES, None, None),
        P(AXES, None, None),
        P(AXES, None),
        P(AXES, None),
        P(AXES),
        P(AXES, None),
        P(AXES, None),
    )
    out_specs = P(AXES, None, None)
    return jax.shard_map(
        per_device, mesh=mesh, in_specs=in_specs, out_specs=out_specs, check_vma=False
    )
```

```python
import functools

import jax
import jax.numpy as jnp
from jax import lax
from jax.experimental import pallas as pl
from jax.experimental.pallas import tpu as pltpu
from jax.sharding import PartitionSpec as P

TILE = 32
LANES = 128
TROWS = TILE * TILE // LANES
ROWS = 16

flow_step = 0.5

PACK_MIB, LADDER_MIB, CROSS_MIB, FINISH_MIB = 40, 20, 40, 50

AXES = ("group", "chan")
X_BITS, Y_BITS, Z_BITS, CORE_BITS = 2, 2, 2, 1
DEVICES = 1 << (X_BITS + Y_BITS + Z_BITS + CORE_BITS)


def device_at(place):
    x = place & ((1 << X_BITS) - 1)
    place = place >> X_BITS
    z = place & ((1 << Z_BITS) - 1)
    place = place >> Z_BITS
    core = place & ((1 << CORE_BITS) - 1)
    y = place >> CORE_BITS
    return (((((x << Y_BITS) | y) << Z_BITS) | z) << CORE_BITS) | core


ORDER = [device_at(place) for place in range(DEVICES)]


def params(mebibytes):
    return pltpu.CompilerParams(vmem_limit_bytes=mebibytes * 1024 * 1024)


def chunks_of(total, count):
    while total % count:
        count -= 1
    return count, total // count


def loop(count, body, unroll=1):
    lax.fori_loop(0, count, lambda i, _: (body(i), 0)[1], 0, unroll=unroll)


def inside_of(first_row, rows, columns, size):
    row = lax.broadcasted_iota(jnp.int32, (rows, columns), 0) + first_row
    column = lax.broadcasted_iota(jnp.int32, (rows, columns), 1)
    return (row < size) & (column < size)


def spread(weight_row, out_ref):
    extent = weight_row.shape[1]
    for k in range(extent // LANES):
        piece = weight_row[:, k * LANES : (k + 1) * LANES]
        out_ref[k * LANES : (k + 1) * LANES, :] = jnp.transpose(
            jnp.broadcast_to(piece, (LANES, LANES))
        )


def pack_kernel(size_hbm, table_hbm, gen_hbm, ham_hbm, out, size_ref, table, words, first_rows, gen, ham, rows, small_sem, in_sem):
    channels, extent, _ = gen.shape
    panels = extent // LANES
    half = rows.shape[0] // 2
    parts = in_sem.shape[1] // channels
    part_rows = extent // parts
    read_table = pltpu.make_async_copy(table_hbm, table, small_sem.at[0])
    read_sizes = pltpu.make_async_copy(size_hbm, size_ref, small_sem.at[1])
    give_rows = pltpu.make_async_copy(words, first_rows, small_sem.at[2])
    read_table.start()
    read_sizes.start()

    def loads(c, h):
        at = pl.ds(h * part_rows, part_rows)
        k = c * parts + h
        return (
            pltpu.make_async_copy(gen_hbm.at[c, at], gen.at[c, at], in_sem.at[0, k]),
            pltpu.make_async_copy(ham_hbm.at[c, at], ham.at[c, at], in_sem.at[1, k]),
        )

    for c in range(channels):
        for h in range(parts):
            for copy in loads(c, h):
                copy.start()
    read_table.wait()
    words[...] = table[...] * TROWS
    give_rows.start()
    read_sizes.wait()
    for c in range(channels):
        size = size_ref[c]
        for h in range(parts):
            for copy in loads(c, h):
                copy.wait()

            def block(b, c=c, h=h, size=size):
                first = pl.multiple_of(h * part_rows + b * ROWS, ROWS)
                inside = inside_of(first, ROWS, extent, size)
                base = (c * extent + first) * panels
                for source, offset in ((gen, 0), (ham, half)):
                    values = source[c, pl.ds(first, ROWS), :].astype(jnp.float32)
                    values = jnp.where(inside, values, 0.0)
                    for p in range(panels):
                        rows[pl.ds(base + (offset + p), ROWS, stride=panels), :] = values[
                            :, p * LANES : (p + 1) * LANES
                        ]

            loop(part_rows // ROWS, block, unroll=2)
    give_rows.wait()

    def pick(slot, row):
        g = rows[pl.ds(row, TROWS), :]
        h = rows[pl.ds(row + half, TROWS), :]
        out[slot] = jnp.concatenate([g, h], axis=0).astype(jnp.bfloat16)

    each_slot(first_rows, 0, DEVICES, pick)


def each_slot(first_rows, start, count, body):
    capacity = first_rows.shape[1] // DEVICES
    for place in range(start, start + count):
        for k in range(capacity):
            row = first_rows[0, ORDER[place] * capacity + k]
            body(place * capacity + k, pl.multiple_of(row, TROWS))


def cross_kernel(table, weight_ref, arrived, out_hbm, words, first_rows, both_rows, gen, ham, wgen, wham, spread_weight, crossed_rows, out, small_sem, out_sem):
    channels, extent = weight_ref.shape
    panels = extent // LANES
    other = both_rows.shape[0] // 2
    parts = out_sem.shape[0]
    part_places = DEVICES // parts
    part_slots = out.shape[0] // parts
    give_rows = pltpu.make_async_copy(words, first_rows, small_sem)

    def place(slot, row):
        both = arrived[slot].astype(jnp.float32)
        both_rows[pl.ds(row, TROWS), :] = both[:TROWS]
        both_rows[pl.ds(row + other, TROWS), :] = both[TROWS:]

    def give(slot, row):
        out[slot] = crossed_rows[pl.ds(row, TROWS), :].astype(jnp.bfloat16)

    def store(q):
        at = pl.ds(q * part_slots, part_slots)
        return pltpu.make_async_copy(out.at[at], out_hbm.at[at], out_sem.at[q])

    words[...] = table[...] * TROWS
    give_rows.start()
    for c in range(channels):
        spread(weight_ref[c : c + 1, :], spread_weight.at[c])
    give_rows.wait()
    each_slot(first_rows, 0, DEVICES, place)

    def relayout(c, first):
        rows = pl.ds(first, ROWS)
        base = (c * extent + first) * panels
        weight = spread_weight[c, rows, :]
        for p in range(0, panels, 2):
            lanes = slice(p * LANES, (p + 2) * LANES)
            g = [both_rows[pl.ds(base + (p + i), ROWS, stride=panels), :] for i in range(2)]
            h = [
                both_rows[pl.ds(base + (other + p + i), ROWS, stride=panels), :]
                for i in range(2)
            ]
            for target, pair in (
                (gen, g),
                (ham, h),
                (wgen, [weight * x for x in g]),
                (wham, [weight * x for x in h]),
            ):
                target[c, rows, lanes] = jnp.concatenate(pair, axis=1).astype(jnp.bfloat16)

    def block(b):
        relayout(0, pl.multiple_of(b * ROWS, ROWS))

    loop(extent // ROWS, block, unroll=2)
    step = 2 * LANES
    for c in range(channels):
        for n in range(extent // step):
            columns = slice(n * step, (n + 1) * step)
            first = jnp.dot(gen[c], wham[c, :, columns], preferred_element_type=jnp.float32)
            second = jnp.dot(ham[c], wgen[c, :, columns], preferred_element_type=jnp.float32)
            product = first - second
            for i in range(step // LANES):
                p = n * (step // LANES) + i
                crossed_rows[
                    pl.ds(c * extent * panels + p, extent, stride=panels), :
                ] = product[:, i * LANES : (i + 1) * LANES]
            if c + 1 < channels:
                for row in range(n * step, (n + 1) * step, ROWS):
                    relayout(c + 1, row)

    for q in range(parts):
        each_slot(first_rows, q * part_places, part_places, give)
        store(q).start()
    for q in range(parts):
        store(q).wait()


def ladder_kernel(size_ref, weight_ref, gen_ref, ham_ref, out_ref, gen, ham, wgen, wham, spread_weight):
    channels, extent, _ = gen_ref.shape
    for c in range(channels):
        size = size_ref[c]
        spread(weight_ref[c : c + 1, :], spread_weight)

        def block(b, c=c, size=size):
            rows = pl.ds(pl.multiple_of(b * ROWS, ROWS), ROWS)
            inside = inside_of(b * ROWS, ROWS, extent, size)
            weight = jnp.tile(spread_weight[rows, :], (1, extent // LANES))
            g = jnp.where(inside, gen_ref[c, rows, :].astype(jnp.float32), 0.0)
            h = jnp.where(inside, ham_ref[c, rows, :].astype(jnp.float32), 0.0)
            gen[rows, :] = g.astype(jnp.bfloat16)
            ham[rows, :] = h.astype(jnp.bfloat16)
            wgen[rows, :] = (weight * g).astype(jnp.bfloat16)
            wham[rows, :] = (weight * h).astype(jnp.bfloat16)

        loop(extent // ROWS, block)
        step = 2 * LANES
        for n in range(extent // step):
            columns = slice(n * step, (n + 1) * step)
            first = jnp.dot(gen[...], wham[:, columns], preferred_element_type=jnp.float32)
            second = jnp.dot(ham[...], wgen[:, columns], preferred_element_type=jnp.float32)
            out_ref[c, :, columns] = ham[:, columns].astype(jnp.float32) + flow_step * (
                first - second
            )


def finish_kernel(size_hbm, table, base_hbm, arrived, out_hbm, size_ref, words, first_rows, base, back_rows, out, small_sem, base_sem, out_sem):
    channels, extent, _ = base.shape
    panels = extent // LANES
    cuts = out_sem.shape[1]
    cut_rows = extent // cuts
    give_rows = pltpu.make_async_copy(words, first_rows, small_sem.at[0])
    read_sizes = pltpu.make_async_copy(size_hbm, size_ref, small_sem.at[1])

    def load_base(c):
        return pltpu.make_async_copy(base_hbm.at[c], base.at[c], base_sem.at[c])

    def store(c, k):
        at = pl.ds(k * cut_rows, cut_rows)
        return pltpu.make_async_copy(out.at[c, at], out_hbm.at[c, at], out_sem.at[c, k])

    def place(slot, row):
        back_rows[pl.ds(row, TROWS), :] = arrived[slot].astype(jnp.float32)

    words[...] = table[...] * TROWS
    give_rows.start()
    read_sizes.start()
    for c in range(channels):
        load_base(c).start()
    give_rows.wait()
    each_slot(first_rows, 0, DEVICES, place)
    read_sizes.wait()
    for c in range(channels):
        size = size_ref[c]
        load_base(c).wait()
        for k in range(cuts):

            def block(b, c=c, k=k, size=size):
                first = pl.multiple_of(k * cut_rows + b * ROWS, ROWS)
                rows = pl.ds(first, ROWS)
                start = (c * extent + first) * panels
                inside = inside_of(first, ROWS, extent, size)
                for p in range(panels):
                    lanes = slice(p * LANES, (p + 1) * LANES)
                    back = back_rows[pl.ds(start + p, ROWS, stride=panels), :]
                    total = base[c, rows, lanes] + flow_step * back
                    out[c, rows, lanes] = jnp.where(inside[:, lanes], total, 0.0)

            loop(cut_rows // ROWS, block, unroll=2)
            store(c, k).start()
    for c in range(channels):
        for k in range(cuts):
            store(c, k).wait()


HBM = functools.partial(pl.BlockSpec, memory_space=pltpu.HBM)
SMEM = functools.partial(pl.BlockSpec, memory_space=pltpu.SMEM)
WHOLE = functools.partial(pl.BlockSpec, memory_space=pltpu.VMEM)


def in_hbm(operand):
    return pltpu.with_memory_space_constraint(operand, pltpu.HBM)


def per_device(
    generator, hamiltonian, pair_weight, cross_weight, channel_size, send_table, receive_table
):
    channels, extent, _ = generator.shape
    slots = send_table.shape[1]
    panels = extent // LANES
    lane_rows = channels * extent * panels + TROWS
    parts = 16
    devices = lax.axis_size(AXES)
    f32, bf16 = jnp.float32, jnp.bfloat16

    outgoing = pl.pallas_call(
        pack_kernel,
        out_shape=jax.ShapeDtypeStruct((slots, 2 * TROWS, LANES), bf16),
        in_specs=[HBM()] * 4,
        out_specs=WHOLE(),
        scratch_shapes=[
            pltpu.SMEM(channel_size.shape, jnp.int32),
            pltpu.VMEM(send_table.shape, jnp.int32),
            pltpu.VMEM((1, slots), jnp.int32),
            pltpu.SMEM((1, slots), jnp.int32),
            pltpu.VMEM((channels, extent, extent), bf16),
            pltpu.VMEM((channels, extent, extent), bf16),
            pltpu.VMEM((2 * lane_rows, LANES), f32),
            pltpu.SemaphoreType.DMA((3,)),
            pltpu.SemaphoreType.DMA((2, 4 * channels)),
        ],
        compiler_params=params(PACK_MIB),
        name="pack",
    )(*(in_hbm(v) for v in (channel_size, send_table, generator, hamiltonian)))

    def exchange(tiles):
        swapped = lax.all_to_all(
            tiles.reshape(devices, slots // devices, *tiles.shape[1:]),
            AXES,
            split_axis=0,
            concat_axis=0,
            tiled=True,
            axis_index_groups=[ORDER],
        )
        return swapped.reshape(tiles.shape)

    arrived = exchange(outgoing)

    base = pl.pallas_call(
        ladder_kernel,
        out_shape=jax.ShapeDtypeStruct((channels, extent, extent), f32),
        in_specs=[SMEM(), WHOLE(), WHOLE(), WHOLE()],
        out_specs=WHOLE(),
        scratch_shapes=[pltpu.VMEM((extent, extent), bf16)] * 4
        + [pltpu.VMEM((extent, LANES), f32)],
        compiler_params=params(LADDER_MIB),
        name="ladder",
    )(channel_size, pair_weight, generator, hamiltonian)

    table_words = [
        pltpu.VMEM((1, slots), jnp.int32),
        pltpu.SMEM((1, slots), jnp.int32),
    ]
    going_back = pl.pallas_call(
        cross_kernel,
        out_shape=jax.ShapeDtypeStruct((slots, TROWS, LANES), bf16),
        in_specs=[WHOLE(), WHOLE(), WHOLE()],
        out_specs=HBM(),
        scratch_shapes=table_words
        + [pltpu.VMEM((2 * lane_rows, LANES), f32)]
        + [pltpu.VMEM((channels, extent, extent), bf16)] * 4
        + [
            pltpu.VMEM((channels, extent, LANES), f32),
            pltpu.VMEM((lane_rows, LANES), f32),
            pltpu.VMEM((slots, TROWS, LANES), bf16),
            pltpu.SemaphoreType.DMA,
            pltpu.SemaphoreType.DMA((parts,)),
        ],
        compiler_params=params(CROSS_MIB),
        name="cross",
    )(receive_table, cross_weight, arrived)

    came_back = exchange(going_back)

    return pl.pallas_call(
        finish_kernel,
        out_shape=jax.ShapeDtypeStruct((channels, extent, extent), f32),
        in_specs=[HBM(), WHOLE(), HBM(), WHOLE()],
        out_specs=HBM(),
        scratch_shapes=[pltpu.SMEM(channel_size.shape, jnp.int32)]
        + table_words
        + [
            pltpu.VMEM((channels, extent, extent), f32),
            pltpu.VMEM((lane_rows, LANES), f32),
            pltpu.VMEM((channels, extent, extent), f32),
            pltpu.SemaphoreType.DMA((2,)),
            pltpu.SemaphoreType.DMA((channels,)),
            pltpu.SemaphoreType.DMA((channels, 4)),
        ],
        compiler_params=params(FINISH_MIB),
        name="finish",
    )(channel_size, send_table, in_hbm(base), came_back)


def solution(mesh):
    in_specs = (
        P(AXES, None, None),
        P(AXES, None, None),
        P(AXES, None),
        P(AXES, None),
        P(AXES),
        P(AXES, None),
        P(AXES, None),
    )
    out_specs = P(AXES, None, None)
    return jax.shard_map(
        per_device, mesh=mesh, in_specs=in_specs, out_specs=out_specs, check_vma=False
    )
```

```python
import functools

import jax
import jax.numpy as jnp
from jax import lax
from jax.experimental import pallas as pl
from jax.experimental.pallas import tpu as pltpu
from jax.sharding import PartitionSpec as P

TILE = 32
LANES = 128
TROWS = TILE * TILE // LANES
ROWS = 16

flow_step = 0.5

PACK_MIB, LADDER_MIB, CROSS_MIB, FINISH_MIB = 40, 20, 40, 50

AXES = ("group", "chan")
X_BITS, Y_BITS, Z_BITS, CORE_BITS = 2, 2, 2, 1
DEVICES = 1 << (X_BITS + Y_BITS + Z_BITS + CORE_BITS)


def device_at(place):
    x = place & ((1 << X_BITS) - 1)
    place = place >> X_BITS
    z = place & ((1 << Z_BITS) - 1)
    place = place >> Z_BITS
    core = place & ((1 << CORE_BITS) - 1)
    y = place >> CORE_BITS
    return (((((x << Y_BITS) | y) << Z_BITS) | z) << CORE_BITS) | core


ORDER = [device_at(place) for place in range(DEVICES)]


def params(mebibytes):
    return pltpu.CompilerParams(vmem_limit_bytes=mebibytes * 1024 * 1024)


def chunks_of(total, count):
    while total % count:
        count -= 1
    return count, total // count


def loop(count, body, unroll=1):
    lax.fori_loop(0, count, lambda i, _: (body(i), 0)[1], 0, unroll=unroll)


def inside_of(first_row, rows, columns, size):
    row = lax.broadcasted_iota(jnp.int32, (rows, columns), 0) + first_row
    column = lax.broadcasted_iota(jnp.int32, (rows, columns), 1)
    return (row < size) & (column < size)


def spread(weight_row, out_ref):
    extent = weight_row.shape[1]
    for k in range(extent // LANES):
        piece = weight_row[:, k * LANES : (k + 1) * LANES]
        out_ref[k * LANES : (k + 1) * LANES, :] = jnp.transpose(
            jnp.broadcast_to(piece, (LANES, LANES))
        )


def pack_kernel(size_hbm, table_hbm, gen_hbm, ham_hbm, out, size_ref, table, words, first_rows, gen, ham, rows, small_sem, in_sem):
    channels, extent, _ = gen.shape
    panels = extent // LANES
    half = rows.shape[0] // 2
    parts = in_sem.shape[1] // channels
    part_rows = extent // parts
    read_table = pltpu.make_async_copy(table_hbm, table, small_sem.at[0])
    read_sizes = pltpu.make_async_copy(size_hbm, size_ref, small_sem.at[1])
    give_rows = pltpu.make_async_copy(words, first_rows, small_sem.at[2])
    read_table.start()
    read_sizes.start()

    def loads(c, h):
        at = pl.ds(h * part_rows, part_rows)
        k = c * parts + h
        return (
            pltpu.make_async_copy(gen_hbm.at[c, at], gen.at[c, at], in_sem.at[0, k]),
            pltpu.make_async_copy(ham_hbm.at[c, at], ham.at[c, at], in_sem.at[1, k]),
        )

    for c in range(channels):
        for h in range(parts):
            for copy in loads(c, h):
                copy.start()
    read_table.wait()
    words[...] = table[...] * TROWS
    give_rows.start()
    read_sizes.wait()
    for c in range(channels):
        size = size_ref[c]
        for h in range(parts):
            for copy in loads(c, h):
                copy.wait()

            def block(b, c=c, h=h, size=size):
                first = pl.multiple_of(h * part_rows + b * ROWS, ROWS)
                inside = inside_of(first, ROWS, extent, size)
                base = (c * extent + first) * panels
                for source, offset in ((gen, 0), (ham, half)):
                    values = source[c, pl.ds(first, ROWS), :].astype(jnp.float32)
                    values = jnp.where(inside, values, 0.0)
                    for p in range(panels):
                        rows[pl.ds(base + (offset + p), ROWS, stride=panels), :] = values[
                            :, p * LANES : (p + 1) * LANES
                        ]

            loop(part_rows // ROWS, block, unroll=2)
    give_rows.wait()

    def pick(slot, row):
        g = rows[pl.ds(row, TROWS), :]
        h = rows[pl.ds(row + half, TROWS), :]
        out[slot] = jnp.concatenate([g, h], axis=0).astype(jnp.bfloat16)

    each_slot(first_rows, 0, DEVICES, pick)


def each_slot(first_rows, start, count, body):
    capacity = first_rows.shape[1] // DEVICES
    for place in range(start, start + count):
        for k in range(capacity):
            row = first_rows[0, ORDER[place] * capacity + k]
            body(place * capacity + k, pl.multiple_of(row, TROWS))


def cross_kernel(table, weight_ref, arrived, out_hbm, words, first_rows, both_rows, gen, ham, wgen, wham, spread_weight, crossed_rows, out, small_sem, out_sem):
    channels, extent = weight_ref.shape
    panels = extent // LANES
    other = both_rows.shape[0] // 2
    parts = out_sem.shape[0]
    part_places = DEVICES // parts
    part_slots = out.shape[0] // parts
    give_rows = pltpu.make_async_copy(words, first_rows, small_sem)

    def place(slot, row):
        both = arrived[slot].astype(jnp.float32)
        both_rows[pl.ds(row, TROWS), :] = both[:TROWS]
        both_rows[pl.ds(row + other, TROWS), :] = both[TROWS:]

    def give(slot, row):
        out[slot] = crossed_rows[pl.ds(row, TROWS), :].astype(jnp.bfloat16)

    def store(q):
        at = pl.ds(q * part_slots, part_slots)
        return pltpu.make_async_copy(out.at[at], out_hbm.at[at], out_sem.at[q])

    words[...] = table[...] * TROWS
    give_rows.start()
    for c in range(channels):
        spread(weight_ref[c : c + 1, :], spread_weight.at[c])
    give_rows.wait()
    each_slot(first_rows, 0, DEVICES, place)

    def relayout(c, first):
        rows = pl.ds(first, ROWS)
        base = (c * extent + first) * panels
        weight = spread_weight[c, rows, :]
        for p in range(0, panels, 2):
            lanes = slice(p * LANES, (p + 2) * LANES)
            g = [both_rows[pl.ds(base + (p + i), ROWS, stride=panels), :] for i in range(2)]
            h = [
                both_rows[pl.ds(base + (other + p + i), ROWS, stride=panels), :]
                for i in range(2)
            ]
            for target, pair in (
                (gen, g),
                (ham, h),
                (wgen, [weight * x for x in g]),
                (wham, [weight * x for x in h]),
            ):
                target[c, rows, lanes] = jnp.concatenate(pair, axis=1).astype(jnp.bfloat16)

    def block(b):
        relayout(0, pl.multiple_of(b * ROWS, ROWS))

    loop(extent // ROWS, block, unroll=2)
    step = 2 * LANES
    for c in range(channels):
        for n in range(extent // step):
            columns = slice(n * step, (n + 1) * step)
            first = jnp.dot(gen[c], wham[c, :, columns], preferred_element_type=jnp.float32)
            second = jnp.dot(ham[c], wgen[c, :, columns], preferred_element_type=jnp.float32)
            product = first - second
            for i in range(step // LANES):
                p = n * (step // LANES) + i
                crossed_rows[
                    pl.ds(c * extent * panels + p, extent, stride=panels), :
                ] = product[:, i * LANES : (i + 1) * LANES]
            if c + 1 < channels:
                for row in range(n * step, (n + 1) * step, ROWS):
                    relayout(c + 1, row)

    for q in range(parts):
        each_slot(first_rows, q * part_places, part_places, give)
        store(q).start()
    for q in range(parts):
        store(q).wait()


def ladder_kernel(size_ref, weight_ref, gen_ref, ham_ref, out_ref, gen, ham, wgen, wham, spread_weight):
    channels, extent, _ = gen_ref.shape
    for c in range(channels):
        size = size_ref[c]
        spread(weight_ref[c : c + 1, :], spread_weight)

        def block(b, c=c, size=size):
            rows = pl.ds(pl.multiple_of(b * ROWS, ROWS), ROWS)
            inside = inside_of(b * ROWS, ROWS, extent, size)
            weight = jnp.tile(spread_weight[rows, :], (1, extent // LANES))
            g = jnp.where(inside, gen_ref[c, rows, :].astype(jnp.float32), 0.0)
            h = jnp.where(inside, ham_ref[c, rows, :].astype(jnp.float32), 0.0)
            gen[rows, :] = g.astype(jnp.bfloat16)
            ham[rows, :] = h.astype(jnp.bfloat16)
            wgen[rows, :] = (weight * g).astype(jnp.bfloat16)
            wham[rows, :] = (weight * h).astype(jnp.bfloat16)

        loop(extent // ROWS, block)
        step = 2 * LANES
        for n in range(extent // step):
            columns = slice(n * step, (n + 1) * step)
            first = jnp.dot(gen[...], wham[:, columns], preferred_element_type=jnp.float32)
            second = jnp.dot(ham[...], wgen[:, columns], preferred_element_type=jnp.float32)
            out_ref[c, :, columns] = ham[:, columns].astype(jnp.float32) + flow_step * (
                first - second
            )


def finish_kernel(size_hbm, table, base_hbm, arrived, out_hbm, size_ref, words, first_rows, base, back_rows, out, small_sem, base_sem, out_sem):
    channels, extent, _ = base.shape
    panels = extent // LANES
    cuts = out_sem.shape[1]
    cut_rows = extent // cuts
    give_rows = pltpu.make_async_copy(words, first_rows, small_sem.at[0])
    read_sizes = pltpu.make_async_copy(size_hbm, size_ref, small_sem.at[1])

    def load_base(c):
        return pltpu.make_async_copy(base_hbm.at[c], base.at[c], base_sem.at[c])

    def store(c, k):
        at = pl.ds(k * cut_rows, cut_rows)
        return pltpu.make_async_copy(out.at[c, at], out_hbm.at[c, at], out_sem.at[c, k])

    def place(slot, row):
        back_rows[pl.ds(row, TROWS), :] = arrived[slot].astype(jnp.float32)

    words[...] = table[...] * TROWS
    give_rows.start()
    read_sizes.start()
    for c in range(channels):
        load_base(c).start()
    give_rows.wait()
    each_slot(first_rows, 0, DEVICES, place)
    read_sizes.wait()
    for c in range(channels):
        size = size_ref[c]
        load_base(c).wait()
        for k in range(cuts):

            def block(b, c=c, k=k, size=size):
                first = pl.multiple_of(k * cut_rows + b * ROWS, ROWS)
                rows = pl.ds(first, ROWS)
                start = (c * extent + first) * panels
                inside = inside_of(first, ROWS, extent, size)
                for p in range(panels):
                    lanes = slice(p * LANES, (p + 1) * LANES)
                    back = back_rows[pl.ds(start + p, ROWS, stride=panels), :]
                    total = base[c, rows, lanes] + flow_step * back
                    out[c, rows, lanes] = jnp.where(inside[:, lanes], total, 0.0)

            loop(cut_rows // ROWS, block, unroll=2)
            store(c, k).start()
    for c in range(channels):
        for k in range(cuts):
            store(c, k).wait()


HBM = functools.partial(pl.BlockSpec, memory_space=pltpu.HBM)
SMEM = functools.partial(pl.BlockSpec, memory_space=pltpu.SMEM)
WHOLE = functools.partial(pl.BlockSpec, memory_space=pltpu.VMEM)


def in_hbm(operand):
    return pltpu.with_memory_space_constraint(operand, pltpu.HBM)


def per_device(
    generator, hamiltonian, pair_weight, cross_weight, channel_size, send_table, receive_table
):
    channels, extent, _ = generator.shape
    slots = send_table.shape[1]
    panels = extent // LANES
    lane_rows = channels * extent * panels + TROWS
    parts = 16
    devices = lax.axis_size(AXES)
    f32, bf16 = jnp.float32, jnp.bfloat16

    outgoing = pl.pallas_call(
        pack_kernel,
        out_shape=jax.ShapeDtypeStruct((slots, 2 * TROWS, LANES), bf16),
        in_specs=[HBM()] * 4,
        out_specs=WHOLE(),
        scratch_shapes=[
            pltpu.SMEM(channel_size.shape, jnp.int32),
            pltpu.VMEM(send_table.shape, jnp.int32),
            pltpu.VMEM((1, slots), jnp.int32),
            pltpu.SMEM((1, slots), jnp.int32),
            pltpu.VMEM((channels, extent, extent), bf16),
            pltpu.VMEM((channels, extent, extent), bf16),
            pltpu.VMEM((2 * lane_rows, LANES), f32),
            pltpu.SemaphoreType.DMA((3,)),
            pltpu.SemaphoreType.DMA((2, 2 * channels)),
        ],
        compiler_params=params(PACK_MIB),
        name="pack",
    )(*(in_hbm(v) for v in (channel_size, send_table, generator, hamiltonian)))

    def exchange(tiles):
        swapped = lax.all_to_all(
            tiles.reshape(devices, slots // devices, *tiles.shape[1:]),
            AXES,
            split_axis=0,
            concat_axis=0,
            tiled=True,
            axis_index_groups=[ORDER],
        )
        return swapped.reshape(tiles.shape)

    arrived = exchange(outgoing)

    base = pl.pallas_call(
        ladder_kernel,
        out_shape=jax.ShapeDtypeStruct((channels, extent, extent), f32),
        in_specs=[SMEM(), WHOLE(), WHOLE(), WHOLE()],
        out_specs=WHOLE(),
        scratch_shapes=[pltpu.VMEM((extent, extent), bf16)] * 4
        + [pltpu.VMEM((extent, LANES), f32)],
        compiler_params=params(LADDER_MIB),
        name="ladder",
    )(channel_size, pair_weight, generator, hamiltonian)

    table_words = [
        pltpu.VMEM((1, slots), jnp.int32),
        pltpu.SMEM((1, slots), jnp.int32),
    ]
    going_back = pl.pallas_call(
        cross_kernel,
        out_shape=jax.ShapeDtypeStruct((slots, TROWS, LANES), bf16),
        in_specs=[WHOLE(), WHOLE(), WHOLE()],
        out_specs=HBM(),
        scratch_shapes=table_words
        + [pltpu.VMEM((2 * lane_rows, LANES), f32)]
        + [pltpu.VMEM((channels, extent, extent), bf16)] * 4
        + [
            pltpu.VMEM((channels, extent, LANES), f32),
            pltpu.VMEM((lane_rows, LANES), f32),
            pltpu.VMEM((slots, TROWS, LANES), bf16),
            pltpu.SemaphoreType.DMA,
            pltpu.SemaphoreType.DMA((parts,)),
        ],
        compiler_params=params(CROSS_MIB),
        name="cross",
    )(receive_table, cross_weight, arrived)

    came_back = exchange(going_back)

    return pl.pallas_call(
        finish_kernel,
        out_shape=jax.ShapeDtypeStruct((channels, extent, extent), f32),
        in_specs=[HBM(), WHOLE(), HBM(), WHOLE()],
        out_specs=HBM(),
        scratch_shapes=[pltpu.SMEM(channel_size.shape, jnp.int32)]
        + table_words
        + [
            pltpu.VMEM((channels, extent, extent), f32),
            pltpu.VMEM((lane_rows, LANES), f32),
            pltpu.VMEM((channels, extent, extent), f32),
            pltpu.SemaphoreType.DMA((2,)),
            pltpu.SemaphoreType.DMA((channels,)),
            pltpu.SemaphoreType.DMA((channels, 4)),
        ],
        compiler_params=params(FINISH_MIB),
        name="finish",
    )(channel_size, send_table, in_hbm(base), came_back)


def solution(mesh):
    in_specs = (
        P(AXES, None, None),
        P(AXES, None, None),
        P(AXES, None),
        P(AXES, None),
        P(AXES),
        P(AXES, None),
        P(AXES, None),
    )
    out_specs = P(AXES, None, None)
    return jax.shard_map(
        per_device, mesh=mesh, in_specs=in_specs, out_specs=out_specs, check_vma=False
    )
```

```python
import functools

import jax
import jax.numpy as jnp
from jax import lax
from jax.experimental import pallas as pl
from jax.experimental.pallas import tpu as pltpu
from jax.sharding import PartitionSpec as P

TILE = 32
LANES = 128
TROWS = TILE * TILE // LANES
ROWS = 16

flow_step = 0.5

PACK_MIB, LADDER_MIB, CROSS_MIB, FINISH_MIB = 40, 20, 40, 50

AXES = ("group", "chan")
X_BITS, Y_BITS, Z_BITS, CORE_BITS = 2, 2, 2, 1
DEVICES = 1 << (X_BITS + Y_BITS + Z_BITS + CORE_BITS)


def device_at(place):
    x = place & ((1 << X_BITS) - 1)
    place = place >> X_BITS
    z = place & ((1 << Z_BITS) - 1)
    place = place >> Z_BITS
    core = place & ((1 << CORE_BITS) - 1)
    y = place >> CORE_BITS
    return (((((x << Y_BITS) | y) << Z_BITS) | z) << CORE_BITS) | core


ORDER = [device_at(place) for place in range(DEVICES)]


def params(mebibytes):
    return pltpu.CompilerParams(vmem_limit_bytes=mebibytes * 1024 * 1024)


def chunks_of(total, count):
    while total % count:
        count -= 1
    return count, total // count


def loop(count, body, unroll=1):
    lax.fori_loop(0, count, lambda i, _: (body(i), 0)[1], 0, unroll=unroll)


def inside_of(first_row, rows, columns, size):
    row = lax.broadcasted_iota(jnp.int32, (rows, columns), 0) + first_row
    column = lax.broadcasted_iota(jnp.int32, (rows, columns), 1)
    return (row < size) & (column < size)


def spread(weight_row, out_ref):
    extent = weight_row.shape[1]
    for k in range(extent // LANES):
        piece = weight_row[:, k * LANES : (k + 1) * LANES]
        out_ref[k * LANES : (k + 1) * LANES, :] = jnp.transpose(
            jnp.broadcast_to(piece, (LANES, LANES))
        )


def pack_kernel(size_hbm, table_hbm, gen_hbm, ham_hbm, out, size_ref, table, words, first_rows, gen, ham, rows, small_sem, in_sem):
    channels, extent, _ = gen.shape
    panels = extent // LANES
    half = rows.shape[0] // 2
    parts = in_sem.shape[1] // channels
    part_rows = extent // parts
    read_table = pltpu.make_async_copy(table_hbm, table, small_sem.at[0])
    read_sizes = pltpu.make_async_copy(size_hbm, size_ref, small_sem.at[1])
    give_rows = pltpu.make_async_copy(words, first_rows, small_sem.at[2])
    read_table.start()
    read_sizes.start()

    def loads(c, h):
        at = pl.ds(h * part_rows, part_rows)
        k = c * parts + h
        return (
            pltpu.make_async_copy(gen_hbm.at[c, at], gen.at[c, at], in_sem.at[0, k]),
            pltpu.make_async_copy(ham_hbm.at[c, at], ham.at[c, at], in_sem.at[1, k]),
        )

    for c in range(channels):
        for h in range(parts):
            for copy in loads(c, h):
                copy.start()
    read_table.wait()
    words[...] = table[...] * TROWS
    give_rows.start()
    read_sizes.wait()
    for c in range(channels):
        size = size_ref[c]
        for h in range(parts):
            for copy in loads(c, h):
                copy.wait()

            def block(b, c=c, h=h, size=size):
                first = pl.multiple_of(h * part_rows + b * ROWS, ROWS)
                inside = inside_of(first, ROWS, extent, size)
                base = (c * extent + first) * panels
                for source, offset in ((gen, 0), (ham, half)):
                    values = source[c, pl.ds(first, ROWS), :].astype(jnp.float32)
                    values = jnp.where(inside, values, 0.0)
                    for p in range(panels):
                        rows[pl.ds(base + (offset + p), ROWS, stride=panels), :] = values[
                            :, p * LANES : (p + 1) * LANES
                        ]

            loop(part_rows // ROWS, block, unroll=2)
    give_rows.wait()

    def pick(slot, row):
        g = rows[pl.ds(row, TROWS), :]
        h = rows[pl.ds(row + half, TROWS), :]
        out[slot] = jnp.concatenate([g, h], axis=0).astype(jnp.bfloat16)

    each_slot(first_rows, 0, DEVICES, pick)


def each_slot(first_rows, start, count, body):
    capacity = first_rows.shape[1] // DEVICES
    for place in range(start, start + count):
        for k in range(capacity):
            row = first_rows[0, ORDER[place] * capacity + k]
            body(place * capacity + k, pl.multiple_of(row, TROWS))


def cross_kernel(table, weight_ref, arrived, out_hbm, words, first_rows, both_rows, left, right, spread_weight, crossed_rows, out, small_sem, out_sem):
    channels, extent = weight_ref.shape
    panels = extent // LANES
    other = both_rows.shape[0] // 2
    parts = out_sem.shape[0]
    part_places = DEVICES // parts
    part_slots = out.shape[0] // parts
    give_rows = pltpu.make_async_copy(words, first_rows, small_sem)

    def place(slot, row):
        both = arrived[slot].astype(jnp.float32)
        both_rows[pl.ds(row, TROWS), :] = both[:TROWS]
        both_rows[pl.ds(row + other, TROWS), :] = both[TROWS:]

    def give(slot, row):
        out[slot] = crossed_rows[pl.ds(row, TROWS), :].astype(jnp.bfloat16)

    def store(q):
        at = pl.ds(q * part_slots, part_slots)
        return pltpu.make_async_copy(out.at[at], out_hbm.at[at], out_sem.at[q])

    words[...] = table[...] * TROWS
    give_rows.start()
    for c in range(channels):
        spread(weight_ref[c : c + 1, :], spread_weight.at[c])
    give_rows.wait()
    each_slot(first_rows, 0, DEVICES, place)

    def relayout(c, first):
        rows = pl.ds(first, ROWS)
        base = (c * extent + first) * panels
        weight = spread_weight[c, rows, :]
        for p in range(0, panels, 2):
            lanes = slice(p * LANES, (p + 2) * LANES)
            g = [both_rows[pl.ds(base + (p + i), ROWS, stride=panels), :] for i in range(2)]
            h = [
                both_rows[pl.ds(base + (other + p + i), ROWS, stride=panels), :]
                for i in range(2)
            ]
            far = slice(extent + p * LANES, extent + (p + 2) * LANES)
            below = pl.ds(first + extent, ROWS)

            def joined(pair):
                return jnp.concatenate(pair, axis=1).astype(jnp.bfloat16)

            left[c, rows, lanes] = joined(g)
            left[c, rows, far] = joined([-x for x in h])
            right[c, rows, lanes] = joined([weight * x for x in h])
            right[c, below, lanes] = joined([weight * x for x in g])

    def block(b):
        relayout(0, pl.multiple_of(b * ROWS, ROWS))

    loop(extent // ROWS, block, unroll=2)
    step = 2 * LANES
    for c in range(channels):
        for n in range(extent // step):
            columns = slice(n * step, (n + 1) * step)
            product = jnp.dot(left[c], right[c, :, columns], preferred_element_type=jnp.float32)
            for i in range(step // LANES):
                p = n * (step // LANES) + i
                crossed_rows[
                    pl.ds(c * extent * panels + p, extent, stride=panels), :
                ] = product[:, i * LANES : (i + 1) * LANES]
            if c + 1 < channels:
                for row in range(n * step, (n + 1) * step, ROWS):
                    relayout(c + 1, row)

    for q in range(parts):
        each_slot(first_rows, q * part_places, part_places, give)
        store(q).start()
    for q in range(parts):
        store(q).wait()


def ladder_kernel(size_ref, weight_ref, gen_ref, ham_ref, out_ref, gen, ham, wgen, wham, spread_weight):
    channels, extent, _ = gen_ref.shape
    for c in range(channels):
        size = size_ref[c]
        spread(weight_ref[c : c + 1, :], spread_weight)

        def block(b, c=c, size=size):
            rows = pl.ds(pl.multiple_of(b * ROWS, ROWS), ROWS)
            inside = inside_of(b * ROWS, ROWS, extent, size)
            weight = jnp.tile(spread_weight[rows, :], (1, extent // LANES))
            g = jnp.where(inside, gen_ref[c, rows, :].astype(jnp.float32), 0.0)
            h = jnp.where(inside, ham_ref[c, rows, :].astype(jnp.float32), 0.0)
            gen[rows, :] = g.astype(jnp.bfloat16)
            ham[rows, :] = h.astype(jnp.bfloat16)
            wgen[rows, :] = (weight * g).astype(jnp.bfloat16)
            wham[rows, :] = (weight * h).astype(jnp.bfloat16)

        loop(extent // ROWS, block)
        step = 2 * LANES
        for n in range(extent // step):
            columns = slice(n * step, (n + 1) * step)
            first = jnp.dot(gen[...], wham[:, columns], preferred_element_type=jnp.float32)
            second = jnp.dot(ham[...], wgen[:, columns], preferred_element_type=jnp.float32)
            out_ref[c, :, columns] = ham[:, columns].astype(jnp.float32) + flow_step * (
                first - second
            )


def finish_kernel(size_hbm, table, base_hbm, arrived, out_hbm, size_ref, words, first_rows, base, back_rows, out, small_sem, base_sem, out_sem):
    channels, extent, _ = base.shape
    panels = extent // LANES
    cuts = out_sem.shape[1]
    cut_rows = extent // cuts
    give_rows = pltpu.make_async_copy(words, first_rows, small_sem.at[0])
    read_sizes = pltpu.make_async_copy(size_hbm, size_ref, small_sem.at[1])

    def load_base(c):
        return pltpu.make_async_copy(base_hbm.at[c], base.at[c], base_sem.at[c])

    def store(c, k):
        at = pl.ds(k * cut_rows, cut_rows)
        return pltpu.make_async_copy(out.at[c, at], out_hbm.at[c, at], out_sem.at[c, k])

    def place(slot, row):
        back_rows[pl.ds(row, TROWS), :] = arrived[slot].astype(jnp.float32)

    words[...] = table[...] * TROWS
    give_rows.start()
    read_sizes.start()
    for c in range(channels):
        load_base(c).start()
    give_rows.wait()
    each_slot(first_rows, 0, DEVICES, place)
    read_sizes.wait()
    for c in range(channels):
        size = size_ref[c]
        load_base(c).wait()
        for k in range(cuts):

            def block(b, c=c, k=k, size=size):
                first = pl.multiple_of(k * cut_rows + b * ROWS, ROWS)
                rows = pl.ds(first, ROWS)
                start = (c * extent + first) * panels
                inside = inside_of(first, ROWS, extent, size)
                for p in range(panels):
                    lanes = slice(p * LANES, (p + 1) * LANES)
                    back = back_rows[pl.ds(start + p, ROWS, stride=panels), :]
                    total = base[c, rows, lanes] + flow_step * back
                    out[c, rows, lanes] = jnp.where(inside[:, lanes], total, 0.0)

            loop(cut_rows // ROWS, block, unroll=2)
            store(c, k).start()
    for c in range(channels):
        for k in range(cuts):
            store(c, k).wait()


HBM = functools.partial(pl.BlockSpec, memory_space=pltpu.HBM)
SMEM = functools.partial(pl.BlockSpec, memory_space=pltpu.SMEM)
WHOLE = functools.partial(pl.BlockSpec, memory_space=pltpu.VMEM)


def in_hbm(operand):
    return pltpu.with_memory_space_constraint(operand, pltpu.HBM)


def per_device(
    generator, hamiltonian, pair_weight, cross_weight, channel_size, send_table, receive_table
):
    channels, extent, _ = generator.shape
    slots = send_table.shape[1]
    panels = extent // LANES
    lane_rows = channels * extent * panels + TROWS
    parts = 16
    devices = lax.axis_size(AXES)
    f32, bf16 = jnp.float32, jnp.bfloat16

    outgoing = pl.pallas_call(
        pack_kernel,
        out_shape=jax.ShapeDtypeStruct((slots, 2 * TROWS, LANES), bf16),
        in_specs=[HBM()] * 4,
        out_specs=WHOLE(),
        scratch_shapes=[
            pltpu.SMEM(channel_size.shape, jnp.int32),
            pltpu.VMEM(send_table.shape, jnp.int32),
            pltpu.VMEM((1, slots), jnp.int32),
            pltpu.SMEM((1, slots), jnp.int32),
            pltpu.VMEM((channels, extent, extent), bf16),
            pltpu.VMEM((channels, extent, extent), bf16),
            pltpu.VMEM((2 * lane_rows, LANES), f32),
            pltpu.SemaphoreType.DMA((3,)),
            pltpu.SemaphoreType.DMA((2, 2 * channels)),
        ],
        compiler_params=params(PACK_MIB),
        name="pack",
    )(*(in_hbm(v) for v in (channel_size, send_table, generator, hamiltonian)))

    def exchange(tiles):
        swapped = lax.all_to_all(
            tiles.reshape(devices, slots // devices, *tiles.shape[1:]),
            AXES,
            split_axis=0,
            concat_axis=0,
            tiled=True,
            axis_index_groups=[ORDER],
        )
        return swapped.reshape(tiles.shape)

    arrived = exchange(outgoing)

    base = pl.pallas_call(
        ladder_kernel,
        out_shape=jax.ShapeDtypeStruct((channels, extent, extent), f32),
        in_specs=[SMEM(), WHOLE(), WHOLE(), WHOLE()],
        out_specs=WHOLE(),
        scratch_shapes=[pltpu.VMEM((extent, extent), bf16)] * 4
        + [pltpu.VMEM((extent, LANES), f32)],
        compiler_params=params(LADDER_MIB),
        name="ladder",
    )(channel_size, pair_weight, generator, hamiltonian)

    table_words = [
        pltpu.VMEM((1, slots), jnp.int32),
        pltpu.SMEM((1, slots), jnp.int32),
    ]
    going_back = pl.pallas_call(
        cross_kernel,
        out_shape=jax.ShapeDtypeStruct((slots, TROWS, LANES), bf16),
        in_specs=[WHOLE(), WHOLE(), WHOLE()],
        out_specs=HBM(),
        scratch_shapes=table_words
        + [pltpu.VMEM((2 * lane_rows, LANES), f32)]
        + [
            pltpu.VMEM((channels, extent, 2 * extent), bf16),
            pltpu.VMEM((channels, 2 * extent, extent), bf16),
        ]
        + [
            pltpu.VMEM((channels, extent, LANES), f32),
            pltpu.VMEM((lane_rows, LANES), f32),
            pltpu.VMEM((slots, TROWS, LANES), bf16),
            pltpu.SemaphoreType.DMA,
            pltpu.SemaphoreType.DMA((parts,)),
        ],
        compiler_params=params(CROSS_MIB),
        name="cross",
    )(receive_table, cross_weight, arrived)

    came_back = exchange(going_back)

    return pl.pallas_call(
        finish_kernel,
        out_shape=jax.ShapeDtypeStruct((channels, extent, extent), f32),
        in_specs=[HBM(), WHOLE(), HBM(), WHOLE()],
        out_specs=HBM(),
        scratch_shapes=[pltpu.SMEM(channel_size.shape, jnp.int32)]
        + table_words
        + [
            pltpu.VMEM((channels, extent, extent), f32),
            pltpu.VMEM((lane_rows, LANES), f32),
            pltpu.VMEM((channels, extent, extent), f32),
            pltpu.SemaphoreType.DMA((2,)),
            pltpu.SemaphoreType.DMA((channels,)),
            pltpu.SemaphoreType.DMA((channels, 4)),
        ],
        compiler_params=params(FINISH_MIB),
        name="finish",
    )(channel_size, send_table, in_hbm(base), came_back)


def solution(mesh):
    in_specs = (
        P(AXES, None, None),
        P(AXES, None, None),
        P(AXES, None),
        P(AXES, None),
        P(AXES),
        P(AXES, None),
        P(AXES, None),
    )
    out_specs = P(AXES, None, None)
    return jax.shard_map(
        per_device, mesh=mesh, in_specs=in_specs, out_specs=out_specs, check_vma=False
    )
```
